256 devices in a mesh: tm: 16 (over y_lo, z), orb: 16 (over y_hi, x, core).
Axes of the slice: x: 4, y: 4 (y_hi: 2, y_lo: 2; y = y_hi * 2 + y_lo), z: 8, core: 2. Of those that a mesh axis runs over, the one named last changes fastest.
Arguments:
- self_energy: float32 [16, 2, 8, 1024, 2048], P('tm', None, None, 'orb'), may hold values from -0.0625 to 0.0625
- history: float32 [16, 2, 1024, 1024], P('tm', None, 'orb'), may hold values from -8 to 8
- memory: int32 [1], replicated, may hold values from 3 to 8
- startup_cut: int32 [16], P('tm'), may hold values from 0 to 2048
- weight_index: int32 [16, 8], P('tm'), may hold values from 0 to 15
- weight_table: float32 [16], replicated, may hold values from 0.3 to 3
Outputs:
- collision: float32 [16, 2048, 1024], P('tm', 'orb')
The draws below stay inside these ranges and needn't reach their ends.
All inputs are finite; a program needn't handle non-finite values.
Results may differ from the reference program's by a relative error of at most 0.0003.
Values sent between devices are 32-bit elements; how exact they have to be, the bound alone decides.
A program may use at most 128 MiB of HBM per device.

```python
import math
import jax
import jax.numpy as jnp
from jax import lax

NORB = 1024
LAGS = 8
R = 2048
NQ = 16
NBLK = 16


def place_ends(drawn, own_key, low, largest):
    spot = [jax.random.randint(jax.random.fold_in(own_key, axis), (), 0, length) for axis, length in enumerate(drawn.shape)]
    main_axis = drawn.shape.index(max(drawn.shape))
    beside = spot[:main_axis] + [(spot[main_axis] + 1) % drawn.shape[main_axis]] + spot[main_axis + 1:]
    return drawn.at[tuple(spot)].set(low).at[tuple(beside)].set(largest)


def strengthened(drawn, own_key, source, target, blocks, factor):
    owner, partner = [(jnp.arange(drawn.shape[dim]) // (drawn.shape[dim] // blocks)).reshape([-1 if axis == dim else 1 for axis in range(drawn.ndim)]) for dim in (source, target)]
    chosen = jax.random.permutation(own_key, blocks)[partner]
    strong = (owner == chosen) | (owner == (partner + blocks // 2) % blocks)
    return jnp.where(strong, factor * drawn, drawn)


def level_of(own_key, dims, split, smallest, high):
    factor_of = 1.0
    for axis_at, parts in split:
        heights = jax.random.uniform(jax.random.fold_in(jax.random.fold_in(own_key, 6), axis_at), (parts,), jnp.float32, smallest / len(split), high / len(split))
        factor_of = factor_of * jnp.repeat(jnp.exp(heights), dims[axis_at] // parts).reshape((-1,) + (1,) * (len(dims) - 1 - axis_at))
    return factor_of


def noise(key, extent, deviation, bound, cuts=(), held_as=jnp.bfloat16):
    entries = deviation * jax.random.normal(key, extent, jnp.float32)
    if cuts:
        entries = entries * level_of(key, extent, cuts, -0.22, 0.18)
    return jnp.clip(entries, -bound, bound).astype(held_as)


def gaussian_with(key, dims, deviation, most, shards, heavy, kind=jnp.bfloat16):
    result = deviation * jax.random.normal(key, dims, jnp.float32)
    if shards:
        result = result * level_of(key, dims, shards, -0.22, 0.18)
    return jnp.clip(strengthened(result, jax.random.fold_in(key, 3), *heavy), -most, most).astype(kind)


def setup_inputs(seed: int = 0) -> dict:
    key_list = jax.random.split(jax.random.key(seed), 7)
    return {
        "self_energy": gaussian_with(key_list[0], (NBLK, 2, LAGS, NORB, R), (2 * NORB * LAGS) ** -0.5, 0.0625, ((0, 16), (3, 16)), (3, 4, 16, 2.0), jnp.float32),
        "history": noise(key_list[1], (NBLK, 2, NORB, NORB), 1.0, 8.0, ((0, 16), (2, 16)), jnp.float32),
        "memory": jax.random.randint(key_list[2], (1,), 3, LAGS + 1).astype(jnp.int32),
        "startup_cut": place_ends(jax.random.randint(key_list[3], (NBLK,), 0, R + 1), jax.random.fold_in(key_list[3], 1), 0, R).astype(jnp.int32),
        "weight_index": place_ends(jax.random.randint(key_list[4], (NBLK, LAGS), 0, NQ), jax.random.fold_in(key_list[4], 1), 0, NQ - 1).astype(jnp.int32),
        "weight_table": jnp.clip(jnp.exp(jax.random.uniform(key_list[5], (NQ,), jnp.float32, math.log(0.3), math.log(3.0))), 0.3, 3.0),
    }


def reference(self_energy, history, memory, startup_cut, weight_index, weight_table):
    padded = jnp.concatenate([jnp.zeros((LAGS - 1, 2, NORB, NORB), jnp.float32), history], axis=0)
    lag_ids = jnp.arange(LAGS, dtype=jnp.int32)[:, None]
    row_ids = jnp.arange(R, dtype=jnp.int32)[None, :]
    table_ids = jnp.arange(NQ, dtype=jnp.int32)[None, :]
    signs = jnp.array([1.0, -1.0], jnp.float32)[:, None, None, None]

    def one_block(block):
        window = lax.dynamic_slice_in_dim(padded, block.astype(jnp.int32), LAGS, 0)
        lagged = jnp.swapaxes(window[::-1], 0, 1)
        chosen = lax.dynamic_index_in_dim(weight_index, block.astype(jnp.int32), 0, keepdims=False)
        weights = jnp.sum(jnp.where(chosen[:, None] == table_ids, weight_table[None, :], jnp.float32(0.0)), axis=1)
        cut_here = lax.dynamic_index_in_dim(startup_cut, block.astype(jnp.int32), 0, keepdims=False)
        last_lag = memory[0] - 1
        kept_mask = (lag_ids < last_lag) | ((lag_ids == last_lag) & (row_ids >= cut_here))
        coef = jnp.where(kept_mask, weights[:, None], jnp.float32(0.0))
        band = lax.dynamic_index_in_dim(self_energy, block.astype(jnp.int32), 0, keepdims=False)
        scaled = band * coef[None, :, None, :] * signs
        return lax.dot_general(scaled, lagged, (((0, 1, 2), (0, 1, 2)), ((), ())), precision=lax.Precision.HIGHEST, preferred_element_type=jnp.float32)

    return lax.map(one_block, jnp.arange(NBLK, dtype=jnp.int32))
```

```python
import functools

import jax
import jax.numpy as jnp
from jax import lax
from jax.experimental import pallas as pl
from jax.experimental.pallas import tpu as pltpu
from jax.sharding import PartitionSpec as P

F32 = jnp.float32
BF16 = jnp.bfloat16
MESH = pl.DeviceIdType.MESH
NT = 16
LAGS = 8
CH = 8
W = 128
ORDER = (2, 1, 3, 0)


def halves(value):
    high = value.astype(BF16)
    return high, (value - high.astype(F32)).astype(BF16)


def kernel(
    mem_ref, cut_ref, index_ref, table_ref, hist_ref, se_ref, out_ref,
    stage, rhs, own_hist, gat, gx, own, oth, core_in, a_in, b_in, c_in, y_in,
    se_sem, g_send, g_recv, k_send, k_recv, a_send, a_recv, b_send, b_recv, c_send, c_recv, y_send, y_recv,
):
    t = lax.axis_index("tm")
    o = lax.axis_index("orb")
    yh, x, core = o // 8, (o // 2) % 4, o % 2

    def orb_of(yh_, x_, core_):
        return yh_ * 8 + x_ * 2 + core_

    up, down = t + 1, t - 1
    partner = (t, orb_of(yh, x, 1 - core))
    right = (t, orb_of(yh, (x + 1) % 4, core))
    left = (t, orb_of(yh, (x + 3) % 4, core))
    across = (t, orb_of(1 - yh, x, core))

    for lag in range(LAGS):
        pltpu.make_async_copy(se_ref.at[0, :, lag], stage.at[lag], se_sem.at[lag]).start()

    barrier = pltpu.get_barrier_semaphore()
    greet = [
        (t <= 14, t + 1), (t >= 1, t - 1), (t <= 8, t + 7), (t >= 7, t - 7),
        (t == 9, 15), (t == 10, 15), (t == 15, 9), (t == 15, 10),
    ]
    count = 4
    for there, who in greet:
        count = count + there.astype(jnp.int32)

        @pl.when(there)
        def _():
            pl.semaphore_signal(barrier, inc=1, device_id=(who, o), device_id_type=MESH)

    for who in (partner, right, left, across):
        pl.semaphore_signal(barrier, inc=1, device_id=who, device_id_type=MESH)

    for c in range(CH):
        own_hist[c] = hist_ref[:, c * W:(c + 1) * W].T
    for lag in range(1, LAGS):

        @pl.when(t < lag)
        def _():
            gat[lag] = jnp.zeros((CH, W, W), F32)

    pl.semaphore_wait(barrier, count)

    def remote(src, dst, send, recv, who):
        return pltpu.make_async_remote_copy(
            src_ref=src, dst_ref=dst, send_sem=send, recv_sem=recv, device_id=who, device_id_type=MESH
        )

    def send_own_up(c):
        return remote(own_hist.at[c], gat.at[1, c], g_send.at[1, c], g_recv.at[1, c], (up, o))

    def send_own_far(c):
        lag = 7 - jnp.maximum(t - 8, 0)
        return remote(own_hist.at[c], gat.at[lag, c], g_send.at[7, c], g_recv.at[lag, c], (jnp.minimum(t + 7, 15), o))

    def relay(lag, c):
        if lag <= 4:
            return remote(gat.at[lag - 1, c], gat.at[lag, c], g_send.at[lag, c], g_recv.at[lag, c], (up, o))
        return remote(gat.at[lag + 1, c], gat.at[lag, c], g_send.at[lag, c], g_recv.at[lag, c], (down, o))

    def relays(lag):
        if lag <= 4:
            return (t <= 14) & (t + 1 >= lag)
        return t - 1 >= lag

    def arrived(lag, c):
        remote(gat.at[lag, c], gat.at[lag, c], g_send.at[lag, c], g_recv.at[lag, c], partner).wait_recv()

    def inside(c):
        return (c >= 0) & (c < CH)

    def take_and_relay(lag, nxt, c):
        @pl.when(inside(c) & (t >= lag))
        def _():
            arrived(lag, c)

        if nxt is not None:

            @pl.when(inside(c) & relays(nxt))
            def _():
                relay(nxt, c).start()

    def to_partner(d, c):
        return remote(oth.at[c, d], core_in.at[c, d], k_send.at[d, c], k_recv.at[d, c], partner)

    def add_partner(d, c):
        to_partner(d, c).wait_recv()
        own[c, d] = own[c, d] + core_in[c, d]

    def a_copy(way, c):
        return remote(own.at[c, 2, way], a_in.at[way, c], a_send.at[way, c], a_recv.at[way, c], (right, left)[way])

    def b_copy(way, c):
        d = (1, 3)[way]
        return remote(own.at[c, d, 1 - way], b_in.at[way, c], b_send.at[way, c], b_recv.at[way, c], (right, left)[way])

    def c_copy(way, c):
        d = (1, 3)[way]
        return remote(own.at[c, d, way], c_in.at[way, c], c_send.at[way, c], c_recv.at[way, c], (right, left)[way])

    def y_copy(c):
        return remote(own.at[c, 0, 1 - yh], y_in.at[c], y_send.at[c], y_recv.at[c], across)

    def prepare(lag):
        pltpu.make_async_copy(se_ref.at[0, :, lag], stage.at[lag], se_sem.at[lag]).wait()
        weight = table_ref[index_ref[0, lag]]
        last = mem_ref[0] - 1
        base = pl.multiple_of(lag * W, W)
        low_base = pl.multiple_of(LAGS * W + lag * W, W)
        for d in range(4):
            for side in range(2):
                for yh_ in range(2):
                    col = pl.multiple_of(yh_ * 1024 + ((x + d) % 4) * 256 + (core if side == 0 else 1 - core) * W, W)
                    rows = col + lax.broadcasted_iota(jnp.int32, (64, W), 1)
                    kept = (lag < last) | ((lag == last) & (rows >= cut_ref[0]))
                    coef = jnp.where(kept, weight, F32(0.0))
                    place = pl.ds((d * 4 + side * 2 + yh_) * W, W)
                    value = jnp.concatenate(
                        [stage[lag, 0, :, pl.ds(col, W)] * coef, -(stage[lag, 1, :, pl.ds(col, W)] * coef)], axis=0
                    )
                    high, low = halves(value)
                    rhs[pl.ds(base, W), place] = high
                    rhs[pl.ds(low_base, W), place] = low

    def load_left(c):
        for lag in range(LAGS):
            high, low = halves(own_hist[c] if lag == 0 else gat[lag, c])
            gx[:W, lag * W:(lag + 1) * W] = high
            gx[W:, lag * W:(lag + 1) * W] = low

    def multiply(d, c):
        cols = pl.ds(d * 512, 512)
        both = jnp.dot(gx[...], rhs[:LAGS * W, cols], preferred_element_type=F32)
        more = jnp.dot(gx[:W], rhs[LAGS * W:, cols], preferred_element_type=F32)
        total = both[:W] + both[W:] + more
        for yh_ in range(2):
            own[c, d, yh_] = total[:, yh_ * W:(yh_ + 1) * W]
            oth[c, d, yh_] = total[:, (2 + yh_) * W:(3 + yh_) * W]
        to_partner(d, c).start()

    def step(s, carry):
        for slot in range(4):
            if slot == 0:

                @pl.when(inside(s + 3) & (t <= 14))
                def _():
                    send_own_up(s + 3).start()

                @pl.when(inside(s + 2) & (t <= 10))
                def _():
                    send_own_far(s + 2).start()

                @pl.when(inside(s - 1))
                def _():
                    c = s - 1
                    add_partner(2, c)
                    a_copy(0, c).start()
                    a_copy(1, c).start()
                    add_partner(1, c)
                    b_copy(0, c).start()
                    add_partner(3, c)
                    b_copy(1, c).start()

                @pl.when(inside(s - 3))
                def _():
                    c = s - 3
                    y_copy(c).wait_recv()
                    total = own[c, 0, yh] + y_in[c]
                    out_ref[:, pl.ds(pl.multiple_of(c * W, W), W)] = total.T

                take_and_relay(4, None, s)
                take_and_relay(5, None, s)

                @pl.when(inside(s))
                def _():
                    load_left(s)

            if slot == 1:
                take_and_relay(3, 4, s + 1)

                @pl.when(inside(s - 1))
                def _():
                    add_partner(0, s - 1)

                @pl.when(inside(s - 2))
                def _():
                    c = s - 2
                    for way in range(2):
                        b_copy(way, c).wait_recv()
                        c_copy(way, c).wait_recv()
                    own[c, 0, 0] = own[c, 0, 0] + (c_in[0, c] + b_in[1, c])
                    own[c, 0, 1] = own[c, 0, 1] + (b_in[0, c] + c_in[1, c])
                    y_copy(c).start()

            if slot == 2:
                take_and_relay(2, 3, s + 2)
                take_and_relay(6, 5, s + 1)

                @pl.when(inside(s - 1))
                def _():
                    c = s - 1
                    for way in range(2):
                        d = (1, 3)[way]
                        a_copy(way, c).wait_recv()
                        own[c, d, way] = own[c, d, way] + a_in[way, c]
                        c_copy(way, c).start()

            if slot == 3:
                take_and_relay(1, 2, s + 3)
                take_and_relay(7, 6, s + 2)

            @pl.when(inside(s))
            def _():
                multiply(ORDER[slot], s)

            lag = (s + 3) * 4 + slot

            @pl.when(lag < LAGS)
            def _():
                prepare(lag)

        return carry

    lax.fori_loop(-3, CH + 3, step, 0)

    def drain(c, carry):
        @pl.when(t <= 14)
        def _():
            send_own_up(c).wait_send()

        @pl.when(t <= 10)
        def _():
            send_own_far(c).wait_send()

        for lag in (2, 3, 4, 5, 6):

            @pl.when(relays(lag))
            def _():
                relay(lag, c).wait_send()

        for d in range(4):
            to_partner(d, c).wait_send()
        for way in range(2):
            a_copy(way, c).wait_send()
            b_copy(way, c).wait_send()
            c_copy(way, c).wait_send()
        y_copy(c).wait_send()
        return carry

    lax.fori_loop(0, CH, drain, 0)


def local(self_energy, history, memory, startup_cut, weight_index, weight_table):
    smem = pl.BlockSpec(memory_space=pltpu.SMEM)
    vmem = pl.BlockSpec(memory_space=pltpu.VMEM)
    dma = pltpu.SemaphoreType.DMA
    piece = (W, W)
    out = pl.pallas_call(
        kernel,
        out_shape=jax.ShapeDtypeStruct((W, CH * W), F32),
        in_specs=[smem, smem, smem, smem, vmem, pl.BlockSpec(memory_space=pl.ANY)],
        out_specs=vmem,
        scratch_shapes=[
            pltpu.VMEM((LAGS, 2, 64, 2048), F32),
            pltpu.VMEM((2 * LAGS * W, 2048), BF16),
            pltpu.VMEM((CH, *piece), F32),
            pltpu.VMEM((LAGS, CH, *piece), F32),
            pltpu.VMEM((2 * W, LAGS * W), BF16),
            pltpu.VMEM((CH, 4, 2, *piece), F32),
            pltpu.VMEM((CH, 4, 2, *piece), F32),
            pltpu.VMEM((CH, 4, 2, *piece), F32),
            pltpu.VMEM((2, CH, *piece), F32),
            pltpu.VMEM((2, CH, *piece), F32),
            pltpu.VMEM((2, CH, *piece), F32),
            pltpu.VMEM((CH, *piece), F32),
            dma((LAGS,)),
            dma((LAGS, CH)), dma((LAGS, CH)),
            dma((4, CH)), dma((4, CH)),
            dma((2, CH)), dma((2, CH)),
            dma((2, CH)), dma((2, CH)),
            dma((2, CH)), dma((2, CH)),
            dma((CH,)), dma((CH,)),
        ],
        compiler_params=pltpu.CompilerParams(
            collective_id=0, has_side_effects=True, vmem_limit_bytes=60 * 1024 * 1024
        ),
        name="collision",
    )(memory, startup_cut, weight_index, weight_table, history.reshape(2 * 64, 1024), self_energy)
    return out[None]


def solution(mesh):
    in_specs = (
        P("tm", None, None, "orb", None),
        P("tm", None, "orb", None),
        P(),
        P("tm"),
        P("tm", None),
        P(),
    )
    out_specs = P("tm", "orb", None)
    return jax.shard_map(local, mesh=mesh, in_specs=in_specs, out_specs=out_specs, check_vma=False)
```

```python
import functools

import jax
import jax.numpy as jnp
from jax import lax
from jax.experimental import pallas as pl
from jax.experimental.pallas import tpu as pltpu
from jax.sharding import PartitionSpec as P

F32 = jnp.float32
BF16 = jnp.bfloat16
MESH = pl.DeviceIdType.MESH
NT = 16
LAGS = 8
CH = 8
W = 128
ORDER = (2, 1, 3, 0)


def halves(value):
    high = value.astype(BF16)
    return high, (value - high.astype(F32)).astype(BF16)


def kernel(
    mem_ref, cut_ref, index_ref, table_ref, hist_ref, se_ref, out_ref,
    stage, rhs, own_hist, gat, via, gx, own, oth, core_in, a_in, b_in, c_in, y_in,
    se_sem, g_send, g_recv, v_recv, k_send, k_recv, a_send, a_recv, b_send, b_recv, c_send, c_recv, y_send, y_recv,
):
    t = lax.axis_index("tm")
    o = lax.axis_index("orb")
    yh, x, core = o // 8, (o // 2) % 4, o % 2

    def orb_of(yh_, x_, core_):
        return yh_ * 8 + x_ * 2 + core_

    up, down = t + 1, t - 1
    partner = (t, orb_of(yh, x, 1 - core))
    right = (t, orb_of(yh, (x + 1) % 4, core))
    left = (t, orb_of(yh, (x + 3) % 4, core))
    across = (t, orb_of(1 - yh, x, core))

    for lag in range(LAGS):
        pltpu.make_async_copy(se_ref.at[0, :, lag], stage.at[lag], se_sem.at[lag]).start()

    barrier = pltpu.get_barrier_semaphore()
    greet = [
        (t <= 14, t + 1), (t >= 1, t - 1), (t <= 6, t + 8), ((t >= 8) & (t <= 14), t - 8),
        (t == 0, 7), (t == 7, 0), ((t >= 8) & (t <= 10), 15), (t == 15, 8), (t == 15, 9), (t == 15, 10),
    ]
    count = 4
    for there, who in greet:
        count = count + there.astype(jnp.int32)

        @pl.when(there)
        def _():
            pl.semaphore_signal(barrier, inc=1, device_id=(who, o), device_id_type=MESH)

    for who in (partner, right, left, across):
        pl.semaphore_signal(barrier, inc=1, device_id=who, device_id_type=MESH)

    for c in range(CH):
        own_hist[c] = hist_ref[:, c * W:(c + 1) * W].T
    for lag in range(1, LAGS):

        @pl.when(t < lag)
        def _():
            gat[lag] = jnp.zeros((CH, W, W), F32)

    pl.semaphore_wait(barrier, count)

    def remote(src, dst, send, recv, who):
        return pltpu.make_async_remote_copy(
            src_ref=src, dst_ref=dst, send_sem=send, recv_sem=recv, device_id=who, device_id_type=MESH
        )

    def send_own_up(c):
        return remote(own_hist.at[c], gat.at[1, c], g_send.at[1, c], g_recv.at[1, c], (up, o))

    def send_own_far(c):
        lag = 7 - jnp.maximum(t - 8, 0)
        return remote(
            own_hist.at[c], gat.at[lag, c], g_send.at[7, c], g_recv.at[lag, c], (jnp.where(t == 0, 7, 15), o)
        )

    far = (t == 0) | ((t >= 8) & (t <= 10))

    def send_own_via(c):
        return remote(own_hist.at[c], via.at[0, c], g_send.at[7, c], v_recv.at[0, c], (down, o))

    def pass_own_via(c):
        return remote(via.at[0, c], gat.at[7, c], g_send.at[0, c], g_recv.at[7, c], (t + 8, o))

    by_via = (t >= 1) & (t <= 7)
    passes = t <= 6

    def relay_via(lag, c):
        return remote(gat.at[lag - 1, c], via.at[lag - 2, c], g_send.at[lag, c], v_recv.at[lag - 2, c], (0, o))

    def pass_relay_via(lag, c):
        return remote(via.at[lag - 2, c], gat.at[lag, c], g_send.at[lag, c], g_recv.at[lag, c], (8, o))

    def relay(lag, c):
        if lag <= 4:
            return remote(gat.at[lag - 1, c], gat.at[lag, c], g_send.at[lag, c], g_recv.at[lag, c], (up, o))
        return remote(gat.at[lag + 1, c], gat.at[lag, c], g_send.at[lag, c], g_recv.at[lag, c], (down, o))

    def relays(lag):
        if lag >= 5:
            return t - 1 >= lag
        return (t <= 14) & (t + 1 >= lag) & ((t != 7) | (lag <= 2))

    def arrived(lag, c):
        remote(gat.at[lag, c], gat.at[lag, c], g_send.at[lag, c], g_recv.at[lag, c], partner).wait_recv()

    def inside(c):
        return (c >= 0) & (c < CH)

    def take_and_relay(lag, nxt, c):
        @pl.when(inside(c) & (t >= lag))
        def _():
            arrived(lag, c)

        if nxt is not None:

            @pl.when(inside(c) & relays(nxt))
            def _():
                relay(nxt, c).start()

        if nxt in (3, 4):

            @pl.when(inside(c) & (t == 7))
            def _():
                relay_via(nxt, c).start()

    def to_partner(d, c):
        return remote(oth.at[c, d], core_in.at[c, d], k_send.at[d, c], k_recv.at[d, c], partner)

    def add_partner(d, c):
        to_partner(d, c).wait_recv()
        own[c, d] = own[c, d] + core_in[c, d]

    def a_copy(way, c):
        return remote(own.at[c, 2, way], a_in.at[way, c], a_send.at[way, c], a_recv.at[way, c], (right, left)[way])

    def b_copy(way, c):
        d = (1, 3)[way]
        return remote(own.at[c, d, 1 - way], b_in.at[way, c], b_send.at[way, c], b_recv.at[way, c], (right, left)[way])

    def c_copy(way, c):
        d = (1, 3)[way]
        return remote(own.at[c, d, way], c_in.at[way, c], c_send.at[way, c], c_recv.at[way, c], (right, left)[way])

    def y_copy(c):
        return remote(own.at[c, 0, 1 - yh], y_in.at[c], y_send.at[c], y_recv.at[c], across)

    def prepare(lag):
        pltpu.make_async_copy(se_ref.at[0, :, lag], stage.at[lag], se_sem.at[lag]).wait()
        weight = table_ref[index_ref[0, lag]]
        last = mem_ref[0] - 1
        base = pl.multiple_of(lag * W, W)
        low_base = pl.multiple_of(LAGS * W + lag * W, W)
        for d in range(4):
            for side in range(2):
                for yh_ in range(2):
                    col = pl.multiple_of(yh_ * 1024 + ((x + d) % 4) * 256 + (core if side == 0 else 1 - core) * W, W)
                    rows = col + lax.broadcasted_iota(jnp.int32, (64, W), 1)
                    kept = (lag < last) | ((lag == last) & (rows >= cut_ref[0]))
                    coef = jnp.where(kept, weight, F32(0.0))
                    place = pl.ds((d * 4 + side * 2 + yh_) * W, W)
                    value = jnp.concatenate(
                        [stage[lag, 0, :, pl.ds(col, W)] * coef, -(stage[lag, 1, :, pl.ds(col, W)] * coef)], axis=0
                    )
                    high, low = halves(value)
                    rhs[pl.ds(base, W), place] = high
                    rhs[pl.ds(low_base, W), place] = low

    def load_left(c):
        for lag in range(LAGS):
            high, low = halves(own_hist[c] if lag == 0 else gat[lag, c])
            gx[:W, lag * W:(lag + 1) * W] = high
            gx[W:, lag * W:(lag + 1) * W] = low

    def multiply(d, c):
        cols = pl.ds(d * 512, 512)
        both = jnp.dot(gx[...], rhs[:LAGS * W, cols], preferred_element_type=F32)
        more = jnp.dot(gx[:W], rhs[LAGS * W:, cols], preferred_element_type=F32)
        total = both[:W] + both[W:] + more
        for yh_ in range(2):
            own[c, d, yh_] = total[:, yh_ * W:(yh_ + 1) * W]
            oth[c, d, yh_] = total[:, (2 + yh_) * W:(3 + yh_) * W]
        to_partner(d, c).start()

    def step(s, carry):
        for slot in range(4):
            if slot == 0:

                @pl.when(inside(s + 3) & (t <= 14))
                def _():
                    send_own_up(s + 3).start()

                @pl.when(inside(s + 3) & far)
                def _():
                    send_own_far(s + 3).start()

                @pl.when(inside(s + 3) & by_via)
                def _():
                    send_own_via(s + 3).start()

                @pl.when(inside(s - 1))
                def _():
                    c = s - 1
                    add_partner(2, c)
                    a_copy(0, c).start()
                    a_copy(1, c).start()
                    add_partner(1, c)
                    b_copy(0, c).start()
                    add_partner(3, c)
                    b_copy(1, c).start()

                @pl.when(inside(s - 3))
                def _():
                    c = s - 3
                    y_copy(c).wait_recv()
                    total = own[c, 0, yh] + y_in[c]
                    out_ref[:, pl.ds(pl.multiple_of(c * W, W), W)] = total.T

                take_and_relay(4, None, s)
                take_and_relay(5, None, s)

                @pl.when(inside(s))
                def _():
                    load_left(s)

            if slot == 1:
                take_and_relay(3, 4, s + 1)

                @pl.when(inside(s - 1))
                def _():
                    add_partner(0, s - 1)

                @pl.when(inside(s - 2))
                def _():
                    c = s - 2
                    for way in range(2):
                        b_copy(way, c).wait_recv()
                        c_copy(way, c).wait_recv()
                    own[c, 0, 0] = own[c, 0, 0] + (c_in[0, c] + b_in[1, c])
                    own[c, 0, 1] = own[c, 0, 1] + (b_in[0, c] + c_in[1, c])
                    y_copy(c).start()

            if slot == 2:
                take_and_relay(2, 3, s + 2)
                take_and_relay(6, 5, s + 1)

                @pl.when(inside(s - 1))
                def _():
                    c = s - 1
                    for way in range(2):
                        d = (1, 3)[way]
                        a_copy(way, c).wait_recv()
                        own[c, d, way] = own[c, d, way] + a_in[way, c]
                        c_copy(way, c).start()

            if slot == 3:
                take_and_relay(1, 2, s + 3)
                take_and_relay(7, 6, s + 2)

                @pl.when(inside(s + 3) & passes)
                def _():
                    send_own_via(s + 3).wait_recv()
                    pass_own_via(s + 3).start()

                for lag in (4, 3):

                    @pl.when(inside(s + 5 - lag) & (t == 0))
                    def _():
                        relay_via(lag, s + 5 - lag).wait_recv()
                        pass_relay_via(lag, s + 5 - lag).start()

            @pl.when(inside(s))
            def _():
                multiply(ORDER[slot], s)

            lag = (s + 3) * 4 + slot

            @pl.when(lag < LAGS)
            def _():
                prepare(lag)

        return carry

    lax.fori_loop(-3, CH + 3, step, 0)

    def drain(c, carry):
        @pl.when(t <= 14)
        def _():
            send_own_up(c).wait_send()

        @pl.when(far)
        def _():
            send_own_far(c).wait_send()

        @pl.when(by_via)
        def _():
            send_own_via(c).wait_send()

        @pl.when(passes)
        def _():
            pass_own_via(c).wait_send()

        for lag in (3, 4):

            @pl.when((t == 0) | (t == 7))
            def _():
                relay_via(lag, c).wait_send()

        for lag in (2, 3, 4, 5, 6):

            @pl.when(relays(lag))
            def _():
                relay(lag, c).wait_send()

        for d in range(4):
            to_partner(d, c).wait_send()
        for way in range(2):
            a_copy(way, c).wait_send()
            b_copy(way, c).wait_send()
            c_copy(way, c).wait_send()
        y_copy(c).wait_send()
        return carry

    lax.fori_loop(0, CH, drain, 0)


def local(self_energy, history, memory, startup_cut, weight_index, weight_table):
    smem = pl.BlockSpec(memory_space=pltpu.SMEM)
    vmem = pl.BlockSpec(memory_space=pltpu.VMEM)
    dma = pltpu.SemaphoreType.DMA
    piece = (W, W)
    out = pl.pallas_call(
        kernel,
        out_shape=jax.ShapeDtypeStruct((W, CH * W), F32),
        in_specs=[smem, smem, smem, smem, vmem, pl.BlockSpec(memory_space=pl.ANY)],
        out_specs=vmem,
        scratch_shapes=[
            pltpu.VMEM((LAGS, 2, 64, 2048), F32),
            pltpu.VMEM((2 * LAGS * W, 2048), BF16),
            pltpu.VMEM((CH, *piece), F32),
            pltpu.VMEM((LAGS, CH, *piece), F32),
            pltpu.VMEM((3, CH, *piece), F32),
            pltpu.VMEM((2 * W, LAGS * W), BF16),
            pltpu.VMEM((CH, 4, 2, *piece), F32),
            pltpu.VMEM((CH, 4, 2, *piece), F32),
            pltpu.VMEM((CH, 4, 2, *piece), F32),
            pltpu.VMEM((2, CH, *piece), F32),
            pltpu.VMEM((2, CH, *piece), F32),
            pltpu.VMEM((2, CH, *piece), F32),
            pltpu.VMEM((CH, *piece), F32),
            dma((LAGS,)),
            dma((LAGS, CH)), dma((LAGS, CH)), dma((3, CH)),
            dma((4, CH)), dma((4, CH)),
            dma((2, CH)), dma((2, CH)),
            dma((2, CH)), dma((2, CH)),
            dma((2, CH)), dma((2, CH)),
            dma((CH,)), dma((CH,)),
        ],
        compiler_params=pltpu.CompilerParams(
            collective_id=0, has_side_effects=True, vmem_limit_bytes=60 * 1024 * 1024
        ),
        name="collision",
    )(memory, startup_cut, weight_index, weight_table, history.reshape(2 * 64, 1024), self_energy)
    return out[None]


def solution(mesh):
    in_specs = (
        P("tm", None, None, "orb", None),
        P("tm", None, "orb", None),
        P(),
        P("tm"),
        P("tm", None),
        P(),
    )
    out_specs = P("tm", "orb", None)
    return jax.shard_map(local, mesh=mesh, in_specs=in_specs, out_specs=out_specs, check_vma=False)
```

```python
import functools

import jax
import jax.numpy as jnp
from jax import lax
from jax.experimental import pallas as pl
from jax.experimental.pallas import tpu as pltpu
from jax.sharding import PartitionSpec as P

F32 = jnp.float32
BF16 = jnp.bfloat16
MESH = pl.DeviceIdType.MESH
NT = 16
LAGS = 8
CH = 8
W = 128
ORDER = (2, 1, 3, 0)
AT = {
    "S1": -24, "D7": -17, "R2": -16, "V": -12, "R6": -11, "R3": -10, "V3": -7, "R4": -5, "R5": -5, "V4": -2,
    "W": 0, "KA": 3, "KB": 4, "K0": 7, "C": 7, "X": 12, "F": 20,
}
PLAN = ("S1", "V", "X", "R5", "R3", "KA", "F", "R6", "C", "KB", "W", "V4", "K0", "R4", "D7", "R2", "V3")


def halves(value):
    high = value.astype(BF16)
    return high, (value - high.astype(F32)).astype(BF16)


def kernel(
    mem_ref, cut_ref, index_ref, table_ref, hist_ref, se_ref, out_ref,
    stage, rhs, own_hist, gat, via, gx, own, oth, core_in, a_in, b_in, c_in, y_in,
    se_sem, g_send, g_recv, v_recv, k_send, k_recv, a_send, a_recv, b_send, b_recv, c_send, c_recv, y_send, y_recv,
):
    t = lax.axis_index("tm")
    o = lax.axis_index("orb")
    yh, x, core = o // 8, (o // 2) % 4, o % 2

    def orb_of(yh_, x_, core_):
        return yh_ * 8 + x_ * 2 + core_

    up, down = t + 1, t - 1
    partner = (t, orb_of(yh, x, 1 - core))
    right = (t, orb_of(yh, (x + 1) % 4, core))
    left = (t, orb_of(yh, (x + 3) % 4, core))
    across = (t, orb_of(1 - yh, x, core))

    for lag in range(LAGS):
        pltpu.make_async_copy(se_ref.at[0, :, lag], stage.at[lag], se_sem.at[lag]).start()

    barrier = pltpu.get_barrier_semaphore()
    greet = [
        (t <= 14, t + 1), (t >= 1, t - 1), (t <= 6, t + 8), ((t >= 8) & (t <= 14), t - 8),
        (t == 0, 7), (t == 7, 0), ((t >= 8) & (t <= 10), 15), (t == 15, 8), (t == 15, 9), (t == 15, 10),
    ]
    count = 4
    for there, who in greet:
        count = count + there.astype(jnp.int32)

        @pl.when(there)
        def _():
            pl.semaphore_signal(barrier, inc=1, device_id=(who, o), device_id_type=MESH)

    for who in (partner, right, left, across):
        pl.semaphore_signal(barrier, inc=1, device_id=who, device_id_type=MESH)

    for c in range(CH):
        own_hist[c] = hist_ref[:, c * W:(c + 1) * W].T
    for lag in range(1, LAGS):

        @pl.when(t < lag)
        def _():
            gat[lag] = jnp.zeros((CH, W, W), F32)

    pl.semaphore_wait(barrier, count)

    def remote(src, dst, send, recv, who):
        return pltpu.make_async_remote_copy(
            src_ref=src, dst_ref=dst, send_sem=send, recv_sem=recv, device_id=who, device_id_type=MESH
        )

    def send_own_up(c):
        return remote(own_hist.at[c], gat.at[1, c], g_send.at[1, c], g_recv.at[1, c], (up, o))

    def send_own_far(c):
        lag = 7 - jnp.maximum(t - 8, 0)
        return remote(
            own_hist.at[c], gat.at[lag, c], g_send.at[7, c], g_recv.at[lag, c], (jnp.where(t == 0, 7, 15), o)
        )

    far = (t == 0) | ((t >= 8) & (t <= 10))

    def send_own_via(c):
        return remote(own_hist.at[c], via.at[0, c], g_send.at[7, c], v_recv.at[0, c], (down, o))

    def pass_own_via(c):
        return remote(via.at[0, c], gat.at[7, c], g_send.at[0, c], g_recv.at[7, c], (t + 8, o))

    by_via = (t >= 1) & (t <= 7)
    passes = t <= 6

    def relay_via(lag, c):
        return remote(gat.at[lag - 1, c], via.at[lag - 2, c], g_send.at[lag, c], v_recv.at[lag - 2, c], (0, o))

    def pass_relay_via(lag, c):
        return remote(via.at[lag - 2, c], gat.at[lag, c], g_send.at[lag, c], g_recv.at[lag, c], (8, o))

    def relay(lag, c):
        if lag <= 4:
            return remote(gat.at[lag - 1, c], gat.at[lag, c], g_send.at[lag, c], g_recv.at[lag, c], (up, o))
        return remote(gat.at[lag + 1, c], gat.at[lag, c], g_send.at[lag, c], g_recv.at[lag, c], (down, o))

    def relays(lag):
        if lag >= 5:
            return t - 1 >= lag
        return (t <= 14) & (t + 1 >= lag) & ((t != 7) | (lag <= 2))

    def arrived(lag, c):
        remote(gat.at[lag, c], gat.at[lag, c], g_send.at[lag, c], g_recv.at[lag, c], partner).wait_recv()

    def inside(c):
        return (c >= 0) & (c < CH)

    def take_and_relay(lag, nxt, c):
        @pl.when(inside(c) & (t >= lag))
        def _():
            arrived(lag, c)

        if nxt is not None:

            @pl.when(inside(c) & relays(nxt))
            def _():
                relay(nxt, c).start()

        if nxt in (3, 4):

            @pl.when(inside(c) & (t == 7))
            def _():
                relay_via(nxt, c).start()

    def to_partner(d, c):
        return remote(oth.at[c, d], core_in.at[c, d], k_send.at[d, c], k_recv.at[d, c], partner)

    def add_partner(d, c):
        to_partner(d, c).wait_recv()
        own[c, d] = own[c, d] + core_in[c, d]

    def a_copy(way, c):
        return remote(own.at[c, 2, way], a_in.at[way, c], a_send.at[way, c], a_recv.at[way, c], (right, left)[way])

    def b_copy(way, c):
        d = (1, 3)[way]
        return remote(own.at[c, d, 1 - way], b_in.at[way, c], b_send.at[way, c], b_recv.at[way, c], (right, left)[way])

    def c_copy(way, c):
        d = (1, 3)[way]
        return remote(own.at[c, d, way], c_in.at[way, c], c_send.at[way, c], c_recv.at[way, c], (right, left)[way])

    def y_copy(c):
        return remote(own.at[c, 0, 1 - yh], y_in.at[c], y_send.at[c], y_recv.at[c], across)

    def prepare(lag):
        pltpu.make_async_copy(se_ref.at[0, :, lag], stage.at[lag], se_sem.at[lag]).wait()
        weight = table_ref[index_ref[0, lag]]
        last = mem_ref[0] - 1
        base = pl.multiple_of(lag * W, W)
        low_base = pl.multiple_of(LAGS * W + lag * W, W)
        for d in range(4):
            for side in range(2):
                for yh_ in range(2):
                    col = pl.multiple_of(yh_ * 1024 + ((x + d) % 4) * 256 + (core if side == 0 else 1 - core) * W, W)
                    rows = col + lax.broadcasted_iota(jnp.int32, (64, W), 1)
                    kept = (lag < last) | ((lag == last) & (rows >= cut_ref[0]))
                    coef = jnp.where(kept, weight, F32(0.0))
                    place = pl.ds((d * 4 + side * 2 + yh_) * W, W)
                    value = jnp.concatenate(
                        [stage[lag, 0, :, pl.ds(col, W)] * coef, -(stage[lag, 1, :, pl.ds(col, W)] * coef)], axis=0
                    )
                    high, low = halves(value)
                    rhs[pl.ds(base, W), place] = high
                    rhs[pl.ds(low_base, W), place] = low

    def load_left(c):
        for lag in range(LAGS):
            high, low = halves(own_hist[c] if lag == 0 else gat[lag, c])
            gx[:W, lag * W:(lag + 1) * W] = high
            gx[W:, lag * W:(lag + 1) * W] = low

    def multiply(d, c):
        cols = pl.ds(d * 512, 512)
        both = jnp.dot(gx[...], rhs[:LAGS * W, cols], preferred_element_type=F32)
        more = jnp.dot(gx[:W], rhs[LAGS * W:, cols], preferred_element_type=F32)
        total = both[:W] + both[W:] + more
        for yh_ in range(2):
            own[c, d, yh_] = total[:, yh_ * W:(yh_ + 1) * W]
            oth[c, d, yh_] = total[:, (2 + yh_) * W:(3 + yh_) * W]
        to_partner(d, c).start()

    def run(name, c):
        def when(cond):
            return pl.when(inside(c) & cond)

        if name == "S1":

            @when(t <= 14)
            def _():
                send_own_up(c).start()

        if name == "D7":

            @when(far)
            def _():
                send_own_far(c).start()

            @when(by_via)
            def _():
                send_own_via(c).start()

        if name == "V":

            @when(passes)
            def _():
                send_own_via(c).wait_recv()
                pass_own_via(c).start()

        if name in ("V3", "V4"):
            lag = int(name[1])

            @when(t == 0)
            def _():
                relay_via(lag, c).wait_recv()
                pass_relay_via(lag, c).start()

        if name in ("R2", "R3", "R4"):
            take_and_relay(int(name[1]) - 1, int(name[1]), c)
        if name in ("R5", "R6"):
            take_and_relay(int(name[1]) + 1, int(name[1]), c)
        if name == "W":
            take_and_relay(4, None, c)
            take_and_relay(5, None, c)

            @pl.when(inside(c))
            def _():
                load_left(c)

        if name == "KA":

            @pl.when(inside(c))
            def _():
                add_partner(2, c)
                a_copy(0, c).start()
                a_copy(1, c).start()

        if name == "KB":

            @pl.when(inside(c))
            def _():
                add_partner(1, c)
                b_copy(0, c).start()
                add_partner(3, c)
                b_copy(1, c).start()

        if name == "K0":

            @pl.when(inside(c))
            def _():
                add_partner(0, c)

        if name == "C":

            @pl.when(inside(c))
            def _():
                for way in range(2):
                    d = (1, 3)[way]
                    a_copy(way, c).wait_recv()
                    own[c, d, way] = own[c, d, way] + a_in[way, c]
                    c_copy(way, c).start()

        if name == "X":

            @pl.when(inside(c))
            def _():
                for way in range(2):
                    b_copy(way, c).wait_recv()
                    c_copy(way, c).wait_recv()
                own[c, 0, 0] = own[c, 0, 0] + (c_in[0, c] + b_in[1, c])
                own[c, 0, 1] = own[c, 0, 1] + (b_in[0, c] + c_in[1, c])
                y_copy(c).start()

        if name == "F":

            @pl.when(inside(c))
            def _():
                y_copy(c).wait_recv()
                total = own[c, 0, yh] + y_in[c]
                out_ref[:, pl.ds(pl.multiple_of(c * W, W), W)] = total.T

    first = min(AT.values()) // 4
    last = CH + max(AT.values()) // 4

    def step(s, carry):
        for slot in range(4):
            for name in PLAN:
                if AT[name] % 4 == slot:
                    run(name, s - AT[name] // 4)

            @pl.when(inside(s))
            def _():
                multiply(ORDER[slot], s)

            lag = (s + 4) * 4 + slot

            @pl.when((lag >= 0) & (lag < LAGS))
            def _():
                prepare(lag)

        return carry

    lax.fori_loop(first, last + 1, step, 0)

    def drain(c, carry):
        @pl.when(t <= 14)
        def _():
            send_own_up(c).wait_send()

        @pl.when(far)
        def _():
            send_own_far(c).wait_send()

        @pl.when(by_via)
        def _():
            send_own_via(c).wait_send()

        @pl.when(passes)
        def _():
            pass_own_via(c).wait_send()

        for lag in (3, 4):

            @pl.when((t == 0) | (t == 7))
            def _():
                relay_via(lag, c).wait_send()

        for lag in (2, 3, 4, 5, 6):

            @pl.when(relays(lag))
            def _():
                relay(lag, c).wait_send()

        for d in range(4):
            to_partner(d, c).wait_send()
        for way in range(2):
            a_copy(way, c).wait_send()
            b_copy(way, c).wait_send()
            c_copy(way, c).wait_send()
        y_copy(c).wait_send()
        return carry

    lax.fori_loop(0, CH, drain, 0)


def local(self_energy, history, memory, startup_cut, weight_index, weight_table):
    smem = pl.BlockSpec(memory_space=pltpu.SMEM)
    vmem = pl.BlockSpec(memory_space=pltpu.VMEM)
    dma = pltpu.SemaphoreType.DMA
    piece = (W, W)
    out = pl.pallas_call(
        kernel,
        out_shape=jax.ShapeDtypeStruct((W, CH * W), F32),
        in_specs=[smem, smem, smem, smem, vmem, pl.BlockSpec(memory_space=pl.ANY)],
        out_specs=vmem,
        scratch_shapes=[
            pltpu.VMEM((LAGS, 2, 64, 2048), F32),
            pltpu.VMEM((2 * LAGS * W, 2048), BF16),
            pltpu.VMEM((CH, *piece), F32),
            pltpu.VMEM((LAGS, CH, *piece), F32),
            pltpu.VMEM((3, CH, *piece), F32),
            pltpu.VMEM((2 * W, LAGS * W), BF16),
            pltpu.VMEM((CH, 4, 2, *piece), F32),
            pltpu.VMEM((CH, 4, 2, *piece), F32),
            pltpu.VMEM((CH, 4, 2, *piece), F32),
            pltpu.VMEM((2, CH, *piece), F32),
            pltpu.VMEM((2, CH, *piece), F32),
            pltpu.VMEM((2, CH, *piece), F32),
            pltpu.VMEM((CH, *piece), F32),
            dma((LAGS,)),
            dma((LAGS, CH)), dma((LAGS, CH)), dma((3, CH)),
            dma((4, CH)), dma((4, CH)),
            dma((2, CH)), dma((2, CH)),
            dma((2, CH)), dma((2, CH)),
            dma((2, CH)), dma((2, CH)),
            dma((CH,)), dma((CH,)),
        ],
        compiler_params=pltpu.CompilerParams(
            collective_id=0, has_side_effects=True, vmem_limit_bytes=60 * 1024 * 1024
        ),
        name="collision",
    )(memory, startup_cut, weight_index, weight_table, history.reshape(2 * 64, 1024), self_energy)
    return out[None]


def solution(mesh):
    in_specs = (
        P("tm", None, None, "orb", None),
        P("tm", None, "orb", None),
        P(),
        P("tm"),
        P("tm", None),
        P(),
    )
    out_specs = P("tm", "orb", None)
    return jax.shard_map(local, mesh=mesh, in_specs=in_specs, out_specs=out_specs, check_vma=False)
```

```python
import functools

import jax
import jax.numpy as jnp
from jax import lax
from jax.experimental import pallas as pl
from jax.experimental.pallas import tpu as pltpu
from jax.sharding import PartitionSpec as P

F32 = jnp.float32
BF16 = jnp.bfloat16
MESH = pl.DeviceIdType.MESH
NT = 16
LAGS = 8
CH = 8
W = 128
ORDER = (2, 1, 3, 0)
AT = {
    "S1": -24, "D7": -11, "R2": -16, "R6": -7, "R3": -10, "R4": -5, "R5": -3, "P1": -22,
    "P2": -12, "W": 0, "KA": 3, "KB": 4, "K0": 11, "C": 6, "X": 12, "F": 16,
}
PLAN = ("X", "KA", "D7", "KB", "P1", "S1", "F", "R3", "W", "K0", "C", "R5", "R4", "P2", "R2", "R6")


def halves(value):
    high = value.astype(BF16)
    return high, (value - high.astype(F32)).astype(BF16)


def kernel(
    mem_ref, cut_ref, index_ref, table_ref, hist_ref, se_ref, out_ref,
    stage, rhs, own_hist, gat, via, gx, own, oth, core_in, a_in, bc_in, y_in,
    se_sem, g_send, g_recv, v_recv, k_send, k_recv, a_send, a_recv, b_send, c_send, bc_recv, y_send, y_recv,
):
    t = lax.axis_index("tm")
    o = lax.axis_index("orb")
    yh, x, core = o // 8, (o // 2) % 4, o % 2

    def orb_of(yh_, x_, core_):
        return yh_ * 8 + x_ * 2 + core_

    up, down = t + 1, t - 1
    partner = (t, orb_of(yh, x, 1 - core))
    right = (t, orb_of(yh, (x + 1) % 4, core))
    left = (t, orb_of(yh, (x + 3) % 4, core))
    across = (t, orb_of(1 - yh, x, core))

    for lag in range(LAGS):
        pltpu.make_async_copy(se_ref.at[0, :, lag], stage.at[lag], se_sem.at[lag]).start()

    barrier = pltpu.get_barrier_semaphore()
    greet = [
        (t <= 14, t + 1), (t >= 1, t - 1), (t <= 8, t + 7), (t >= 7, t - 7),
        ((t == 9) | (t == 10), 15), (t == 15, 9), (t == 15, 10),
        ((t == 1) | (t == 2), 7), (t == 7, 1), (t == 7, 2), (t == 7, 15), (t == 15, 7),
    ]
    count = 4
    for there, who in greet:
        count = count + there.astype(jnp.int32)

        @pl.when(there)
        def _():
            pl.semaphore_signal(barrier, inc=1, device_id=(who, o), device_id_type=MESH)

    for who in (partner, right, left, across):
        pl.semaphore_signal(barrier, inc=1, device_id=who, device_id_type=MESH)

    for c in range(CH):
        own_hist[c] = hist_ref[:, c * W:(c + 1) * W].T
    for lag in range(1, LAGS):

        @pl.when(t < lag)
        def _():
            gat[lag] = jnp.zeros((CH, W, W), F32)

    pl.semaphore_wait(barrier, count)

    def remote(src, dst, send, recv, who):
        return pltpu.make_async_remote_copy(
            src_ref=src, dst_ref=dst, send_sem=send, recv_sem=recv, device_id=who, device_id_type=MESH
        )

    def go(make, c):
        @pl.when(c >= 2)
        def _():
            make(c - 2).wait_send()

        make(c).start()

    def history(src, lag, c, kind, who):
        return remote(src, gat.at[lag, c], g_send.at[kind, c % 2], g_recv.at[lag, c], (who, o))

    def send_own_up(c):
        return history(own_hist.at[c], 1, c, 1, up)

    def relay(lag, c):
        if lag <= 4:
            return history(gat.at[lag - 1, c], lag, c, lag, up)
        return history(gat.at[lag + 1, c], lag, c, lag, down)

    def send_own_far(c):
        return history(own_hist.at[c], 7 - jnp.maximum(t - 8, 0), c, 7, jnp.minimum(t + 7, 15))

    def send_own_seven(c):
        return history(own_hist.at[c], 7 - t, c, 6, 7)

    def relay_via(lag, c):
        src = own_hist.at[c] if lag == 1 else gat.at[1, c]
        return remote(src, via.at[lag - 1, c], g_send.at[lag, c % 2], v_recv.at[lag - 1, c], (15, o))

    def pass_via(lag, c):
        return history(via.at[lag - 1, c], lag, c, lag, 8)

    def relays(lag):
        if lag >= 5:
            return (t - 1 >= lag) & (t != 8)
        return (t <= 14) & (t + 1 >= lag) & ((t != 7) | (lag >= 3))

    def arrived(lag, c):
        remote(gat.at[lag, c], gat.at[lag, c], g_send.at[lag, 0], g_recv.at[lag, c], partner).wait_recv()

    def inside(c):
        return (c >= 0) & (c < CH)

    def take_and_relay(lag, nxt, c):
        @pl.when(inside(c) & (t >= lag))
        def _():
            arrived(lag, c)

        if nxt is not None:

            @pl.when(inside(c) & relays(nxt))
            def _():
                go(functools.partial(relay, nxt), c)

        if nxt == 2:

            @pl.when(inside(c) & (t == 7))
            def _():
                go(functools.partial(relay_via, 2), c)

    def to_partner(q, c):
        return remote(oth.at[c, q], core_in.at[c, q], k_send.at[q, c % 2], k_recv.at[(0, 1, 1, 2)[q], c], partner)

    def add_partner(start, size, c):
        part = core_in.at[c, pl.ds(start, size)]
        remote(part, part, k_send.at[start, c % 2], k_recv.at[(0, 1, 1, 2)[start], c], partner).wait_recv()
        own[c, pl.ds(start, size)] = own[c, pl.ds(start, size)] + core_in[c, pl.ds(start, size)]

    def a_copy(way, c):
        return remote(own.at[c, 0, way], a_in.at[c, way], a_send.at[way, c % 2], a_recv.at[c], (right, left)[way])

    def b_copy(way, c):
        return remote(
            own.at[c, 1 + way, 1 - way], bc_in.at[c, way], b_send.at[way, c % 2], bc_recv.at[c], (right, left)[way]
        )

    def c_copy(way, c):
        return remote(
            own.at[c, 1 + way, way], bc_in.at[c, 2 + way], c_send.at[way, c % 2], bc_recv.at[c], (right, left)[way]
        )

    def y_copy(c):
        return remote(own.at[c, 3, 1 - yh], y_in.at[c], y_send.at[c % 2], y_recv.at[c], across)

    def prepare(lag):
        pltpu.make_async_copy(se_ref.at[0, :, lag], stage.at[lag], se_sem.at[lag]).wait()
        weight = table_ref[index_ref[0, lag]]
        last = mem_ref[0] - 1
        base = pl.multiple_of(lag * W, W)
        low_base = pl.multiple_of(LAGS * W + lag * W, W)
        for q, d in enumerate(ORDER):
            for side in range(2):
                for yh_ in range(2):
                    col = pl.multiple_of(yh_ * 1024 + ((x + d) % 4) * 256 + (core if side == 0 else 1 - core) * W, W)
                    rows = col + lax.broadcasted_iota(jnp.int32, (64, W), 1)
                    kept = (lag < last) | ((lag == last) & (rows >= cut_ref[0]))
                    coef = jnp.where(kept, weight, F32(0.0))
                    place = pl.ds((q * 4 + side * 2 + yh_) * W, W)
                    value = jnp.concatenate(
                        [stage[lag, 0, :, pl.ds(col, W)] * coef, -(stage[lag, 1, :, pl.ds(col, W)] * coef)], axis=0
                    )
                    high, low = halves(value)
                    rhs[pl.ds(base, W), place] = high
                    rhs[pl.ds(low_base, W), place] = low

    def load_left(c):
        for lag in range(LAGS):
            high, low = halves(own_hist[c] if lag == 0 else gat[lag, c])
            gx[:W, lag * W:(lag + 1) * W] = high
            gx[W:, lag * W:(lag + 1) * W] = low

    def multiply(q, c):
        cols = pl.ds(q * 512, 512)
        both = jnp.dot(gx[...], rhs[:LAGS * W, cols], preferred_element_type=F32)
        more = jnp.dot(gx[:W], rhs[LAGS * W:, cols], preferred_element_type=F32)
        total = both[:W] + both[W:] + more
        for yh_ in range(2):
            own[c, q, yh_] = total[:, yh_ * W:(yh_ + 1) * W]
            oth[c, q, yh_] = total[:, (2 + yh_) * W:(3 + yh_) * W]
        go(functools.partial(to_partner, q), c)

    def run(name, c):
        def when(cond):
            return pl.when(inside(c) & cond)

        if name == "S1":

            @when((t <= 14) & (t != 7))
            def _():
                go(send_own_up, c)

            @when(t == 7)
            def _():
                go(functools.partial(relay_via, 1), c)

        if name == "D7":

            @when(t <= 10)
            def _():
                go(send_own_far, c)

            @when((t == 1) | (t == 2))
            def _():
                go(send_own_seven, c)

        if name in ("P1", "P2"):
            lag = int(name[1])

            @when(t == 15)
            def _():
                relay_via(lag, c).wait_recv()
                go(functools.partial(pass_via, lag), c)

        if name in ("R2", "R3", "R4"):
            take_and_relay(int(name[1]) - 1, int(name[1]), c)
        if name in ("R5", "R6"):
            take_and_relay(int(name[1]) + 1, int(name[1]), c)
        if name == "W":
            take_and_relay(4, None, c)
            take_and_relay(5, None, c)

            @pl.when(inside(c))
            def _():
                load_left(c)

        if name == "KA":

            @pl.when(inside(c))
            def _():
                add_partner(0, 1, c)
                for way in range(2):
                    go(functools.partial(a_copy, way), c)

        if name == "KB":

            @pl.when(inside(c))
            def _():
                add_partner(1, 2, c)
                for way in range(2):
                    go(functools.partial(b_copy, way), c)

        if name == "K0":

            @pl.when(inside(c))
            def _():
                add_partner(3, 1, c)

        if name == "C":

            @pl.when(inside(c))
            def _():
                remote(a_in.at[c], a_in.at[c], a_send.at[0, 0], a_recv.at[c], left).wait_recv()
                for way in range(2):
                    own[c, 1 + way, way] = own[c, 1 + way, way] + a_in[c, way]
                    go(functools.partial(c_copy, way), c)

        if name == "X":

            @pl.when(inside(c))
            def _():
                remote(bc_in.at[c], bc_in.at[c], b_send.at[0, 0], bc_recv.at[c], left).wait_recv()
                own[c, 3, 0] = own[c, 3, 0] + (bc_in[c, 2] + bc_in[c, 1])
                own[c, 3, 1] = own[c, 3, 1] + (bc_in[c, 0] + bc_in[c, 3])
                go(y_copy, c)

        if name == "F":

            @pl.when(inside(c))
            def _():
                y_copy(c).wait_recv()
                total = own[c, 3, yh] + y_in[c]
                out_ref[:, pl.ds(pl.multiple_of(c * W, W), W)] = total.T

    first = min(AT.values()) // 4
    last = CH + max(AT.values()) // 4

    def step(s, carry):
        for slot in range(4):
            for name in PLAN:
                if AT[name] % 4 == slot:
                    run(name, s - AT[name] // 4)

            @pl.when(inside(s))
            def _():
                multiply(slot, s)

            lag = (s + 4) * 4 + slot

            @pl.when((lag >= 0) & (lag < LAGS))
            def _():
                prepare(lag)

        return carry

    lax.fori_loop(first, last + 1, step, 0)

    for c in (CH - 2, CH - 1):
        ends = [
            ((t <= 14) & (t != 7), send_own_up), (t == 7, functools.partial(relay_via, 1)),
            (t == 7, functools.partial(relay_via, 2)), (t <= 10, send_own_far),
            ((t == 1) | (t == 2), send_own_seven),
            (t == 15, functools.partial(pass_via, 1)), (t == 15, functools.partial(pass_via, 2)),
        ] + [(relays(lag), functools.partial(relay, lag)) for lag in range(2, 7)]
        for there, make in ends:

            @pl.when(there)
            def _():
                make(c).wait_send()

        for q in range(4):
            to_partner(q, c).wait_send()
        for way in range(2):
            for make in (a_copy, b_copy, c_copy):
                make(way, c).wait_send()
        y_copy(c).wait_send()


def local(self_energy, history, memory, startup_cut, weight_index, weight_table):
    smem = pl.BlockSpec(memory_space=pltpu.SMEM)
    vmem = pl.BlockSpec(memory_space=pltpu.VMEM)
    dma = pltpu.SemaphoreType.DMA
    piece = (W, W)
    out = pl.pallas_call(
        kernel,
        out_shape=jax.ShapeDtypeStruct((W, CH * W), F32),
        in_specs=[smem, smem, smem, smem, vmem, pl.BlockSpec(memory_space=pl.ANY)],
        out_specs=vmem,
        scratch_shapes=[
            pltpu.VMEM((LAGS, 2, 64, 2048), F32),
            pltpu.VMEM((2 * LAGS * W, 2048), BF16),
            pltpu.VMEM((CH, *piece), F32),
            pltpu.VMEM((LAGS, CH, *piece), F32),
            pltpu.VMEM((2, CH, *piece), F32),
            pltpu.VMEM((2 * W, LAGS * W), BF16),
            pltpu.VMEM((CH, 4, 2, *piece), F32),
            pltpu.VMEM((CH, 4, 2, *piece), F32),
            pltpu.VMEM((CH, 4, 2, *piece), F32),
            pltpu.VMEM((CH, 2, *piece), F32),
            pltpu.VMEM((CH, 4, *piece), F32),
            pltpu.VMEM((CH, *piece), F32),
            dma((LAGS,)),
            dma((LAGS, 2)), dma((LAGS, CH)), dma((2, CH)),
            dma((4, 2)), dma((3, CH)),
            dma((2, 2)), dma((CH,)),
            dma((2, 2)), dma((2, 2)), dma((CH,)),
            dma((2,)), dma((CH,)),
        ],
        compiler_params=pltpu.CompilerParams(
            collective_id=0, has_side_effects=True, vmem_limit_bytes=60 * 1024 * 1024
        ),
        name="collision",
    )(memory, startup_cut, weight_index, weight_table, history.reshape(2 * 64, 1024), self_energy)
    return out[None]


def solution(mesh):
    in_specs = (
        P("tm", None, None, "orb", None),
        P("tm", None, "orb", None),
        P(),
        P("tm"),
        P("tm", None),
        P(),
    )
    out_specs = P("tm", "orb", None)
    return jax.shard_map(local, mesh=mesh, in_specs=in_specs, out_specs=out_specs, check_vma=False)
```

```python
import functools

import jax
import jax.numpy as jnp
from jax import lax
from jax.experimental import pallas as pl
from jax.experimental.pallas import tpu as pltpu
from jax.sharding import PartitionSpec as P

F32 = jnp.float32
BF16 = jnp.bfloat16
MESH = pl.DeviceIdType.MESH
NT = 16
LAGS = 8
CH = 8
W = 128
ZERO = 16
ORDER = (2, 1, 3, 0)
PLANS = {
    3: (
        {
            "S1": -10, "R2": -5, "R3": 0, "W": 0, "KA": 3, "KB": 4, "K0": 8, "C": 7,
            "X": 12, "F": 18,
        },
        ("F", "X", "R3", "KA", "C", "R2", "S1", "W", "K0", "KB"),
    ),
    4: (
        {
            "S1": -14, "R2": -10, "R3": -5, "R4": 0, "P1": -11, "W": 0, "KA": 2, "KB": 4,
            "K0": 6, "C": 7, "X": 14, "F": 19,
        },
        ("S1", "C", "R2", "KB", "P1", "F", "K0", "R3", "X", "KA", "R4", "W"),
    ),
    5: (
        {
            "S1": -21, "R2": -13, "R3": -7, "R4": -3, "P1": -18, "P2": -9, "W": 0, "KA": 2,
            "KB": 4, "K0": 7, "C": 5, "X": 10, "F": 15,
        },
        ("KB", "S1", "X", "F", "C", "R4", "P1", "R3", "W", "P2", "K0", "KA", "R2"),
    ),
    8: (
        {
            "S1": -24, "D7": -11, "R2": -16, "R6": -7, "R3": -10, "R4": -5, "R5": -3, "P1": -22,
            "P2": -12, "W": 0, "KA": 3, "KB": 4, "K0": 11, "C": 6, "X": 12, "F": 16,
        },
        ("X", "KA", "D7", "KB", "P1", "S1", "F", "R3", "W", "K0", "C", "R5", "R4", "P2", "R2", "R6"),
    ),
}


def halves(value):
    high = value.astype(BF16)
    return high, (value - high.astype(F32)).astype(BF16)


def kernel(
    keep, mem_ref, cut_ref, index_ref, table_ref, hist_ref, se_ref, out_ref,
    stage, rhs, own_hist, gat, via, gx, own, oth, core_in, a_in, bc_in, y_in,
    se_sem, g_send, g_recv, v_recv, k_send, k_recv, a_send, a_recv, b_send, c_send, bc_recv, y_send, y_recv,
):
    ups = min(4, keep - 1)
    downs = keep > 5
    by_via = {3: (), 4: (1,)}.get(keep, (1, 2))
    AT, PLAN = PLANS[keep]
    t = lax.axis_index("tm")
    o = lax.axis_index("orb")
    yh, x, core = o // 8, (o // 2) % 4, o % 2

    def orb_of(yh_, x_, core_):
        return yh_ * 8 + x_ * 2 + core_

    up, down = t + 1, t - 1
    partner = (t, orb_of(yh, x, 1 - core))
    right = (t, orb_of(yh, (x + 1) % 4, core))
    left = (t, orb_of(yh, (x + 3) % 4, core))
    across = (t, orb_of(1 - yh, x, core))

    for lag in range(keep):
        pltpu.make_async_copy(se_ref.at[0, :, lag], stage.at[lag], se_sem.at[lag]).start()

    barrier = pltpu.get_barrier_semaphore()
    greet = [(t <= 14, t + 1), (t >= 1, t - 1)]
    if by_via:
        greet += [(t == 7, 15), (t == 15, 7), (t == 15, 8), (t == 8, 15)]
    if downs:
        greet += [
            (t <= 7, t + 7), ((t >= 7) & (t <= 14), t - 7),
            ((t == 9) | (t == 10), 15), (t == 15, 9), (t == 15, 10),
            ((t == 1) | (t == 2), 7), (t == 7, 1), (t == 7, 2),
        ]
    count = 4
    for there, who in greet:
        count = count + there.astype(jnp.int32)

        @pl.when(there)
        def _():
            pl.semaphore_signal(barrier, inc=1, device_id=(who, o), device_id_type=MESH)

    for who in (partner, right, left, across):
        pl.semaphore_signal(barrier, inc=1, device_id=who, device_id_type=MESH)

    for c in range(CH):
        own_hist[c] = hist_ref[:, c * W:(c + 1) * W].T
    for lag in range(1, keep):

        @pl.when(t < lag)
        def _():
            gat[lag] = jnp.zeros((CH, W, W), F32)

    pl.semaphore_wait(barrier, count)

    def remote(src, dst, send, recv, who):
        return pltpu.make_async_remote_copy(
            src_ref=src, dst_ref=dst, send_sem=send, recv_sem=recv, device_id=who, device_id_type=MESH
        )

    def go(make, c):
        @pl.when(c >= 2)
        def _():
            make(c - 2).wait_send()

        make(c).start()

    def history(src, lag, c, kind, who):
        return remote(src, gat.at[lag, c], g_send.at[kind, c % 2], g_recv.at[lag, c], (who, o))

    def send_own_up(c):
        return history(own_hist.at[c], 1, c, 1, up)

    def relay(lag, c):
        if lag <= 4:
            return history(gat.at[lag - 1, c], lag, c, lag, up)
        return history(gat.at[lag + 1, c], lag, c, lag, down)

    def send_own_far(c):
        return history(own_hist.at[c], 7 - jnp.maximum(t - 8, 0), c, 7, jnp.minimum(t + 7, 15))

    def send_own_seven(c):
        return history(own_hist.at[c], 7 - t, c, 6, 7)

    def relay_via(lag, c):
        src = own_hist.at[c] if lag == 1 else gat.at[1, c]
        return remote(src, via.at[lag - 1, c], g_send.at[lag, c % 2], v_recv.at[lag - 1, c], (15, o))

    def pass_via(lag, c):
        return history(via.at[lag - 1, c], lag, c, lag, 8)

    def comes(lag):
        return lag <= ups if lag <= 4 else downs

    def relays(lag):
        if lag >= 5:
            return (t - 1 >= lag) & (t != 8)
        if lag in by_via:
            return (t <= 14) & (t + 1 >= lag) & (t != 7)
        return (t <= 14) & (t + 1 >= lag)

    def arrived(lag, c):
        remote(gat.at[lag, c], gat.at[lag, c], g_send.at[lag, 0], g_recv.at[lag, c], partner).wait_recv()

    def inside(at):
        return (at >= ZERO) & (at < ZERO + CH)

    def chunk_of(at):
        return jnp.clip(at, ZERO, ZERO + CH - 1) - ZERO

    def take_and_relay(there, lag, nxt, c):
        if comes(lag):

            @pl.when(there & (t >= lag))
            def _():
                arrived(lag, c)

        if nxt is not None and comes(nxt):

            @pl.when(there & relays(nxt))
            def _():
                go(functools.partial(relay, nxt), c)

            if nxt in by_via:

                @pl.when(there & (t == 7))
                def _():
                    go(functools.partial(relay_via, nxt), c)

    def to_partner(q, c):
        return remote(oth.at[c, q], core_in.at[c, q], k_send.at[q, c % 2], k_recv.at[(0, 1, 1, 2)[q], c], partner)

    def add_partner(start, size, c):
        part = core_in.at[c, pl.ds(start, size)]
        remote(part, part, k_send.at[start, c % 2], k_recv.at[(0, 1, 1, 2)[start], c], partner).wait_recv()
        own[c, pl.ds(start, size)] = own[c, pl.ds(start, size)] + core_in[c, pl.ds(start, size)]

    def a_copy(way, c):
        return remote(own.at[c, 0, way], a_in.at[c, way], a_send.at[way, c % 2], a_recv.at[c], (right, left)[way])

    def b_copy(way, c):
        return remote(
            own.at[c, 1 + way, 1 - way], bc_in.at[c, way], b_send.at[way, c % 2], bc_recv.at[c], (right, left)[way]
        )

    def c_copy(way, c):
        return remote(
            own.at[c, 1 + way, way], bc_in.at[c, 2 + way], c_send.at[way, c % 2], bc_recv.at[c], (right, left)[way]
        )

    def y_copy(c):
        return remote(own.at[c, 3, 1 - yh], y_in.at[c], y_send.at[c % 2], y_recv.at[c], across)

    def prepare(lag):
        pltpu.make_async_copy(se_ref.at[0, :, lag], stage.at[lag], se_sem.at[lag]).wait()
        weight = table_ref[index_ref[0, lag]]
        last = mem_ref[0] - 1
        base = pl.multiple_of(lag * W, W)
        low_base = pl.multiple_of(keep * W + lag * W, W)
        for q, d in enumerate(ORDER):
            for side in range(2):
                for yh_ in range(2):
                    col = pl.multiple_of(yh_ * 1024 + ((x + d) % 4) * 256 + (core if side == 0 else 1 - core) * W, W)
                    rows = col + lax.broadcasted_iota(jnp.int32, (64, W), 1)
                    kept = (lag < last) | ((lag == last) & (rows >= cut_ref[0]))
                    coef = jnp.where(kept, weight, F32(0.0))
                    place = pl.ds((q * 4 + side * 2 + yh_) * W, W)
                    value = jnp.concatenate(
                        [stage[lag, 0, :, pl.ds(col, W)] * coef, -(stage[lag, 1, :, pl.ds(col, W)] * coef)], axis=0
                    )
                    high, low = halves(value)
                    rhs[pl.ds(base, W), place] = high
                    rhs[pl.ds(low_base, W), place] = low

    def load_left(c):
        for lag in range(keep):
            high, low = halves(own_hist[c] if lag == 0 else gat[lag, c])
            gx[:W, lag * W:(lag + 1) * W] = high
            gx[W:, lag * W:(lag + 1) * W] = low

    def multiply(q, c):
        cols = pl.ds(q * 512, 512)
        both = jnp.dot(gx[...], rhs[:keep * W, cols], preferred_element_type=F32)
        more = jnp.dot(gx[:W], rhs[keep * W:, cols], preferred_element_type=F32)
        total = both[:W] + both[W:] + more
        for yh_ in range(2):
            own[c, q, yh_] = total[:, yh_ * W:(yh_ + 1) * W]
            oth[c, q, yh_] = total[:, (2 + yh_) * W:(3 + yh_) * W]
        go(functools.partial(to_partner, q), c)

    def run(name, at):
        there = inside(at)
        c = chunk_of(at)

        def when(cond):
            return pl.when(there & cond)

        if name == "S1":

            @when(relays(1))
            def _():
                go(send_own_up, c)

            if 1 in by_via:

                @when(t == 7)
                def _():
                    go(functools.partial(relay_via, 1), c)

        if name == "D7" and downs:

            @when(t <= 10)
            def _():
                go(send_own_far, c)

            @when((t == 1) | (t == 2))
            def _():
                go(send_own_seven, c)

        if name in ("P1", "P2") and int(name[1]) in by_via:
            lag = int(name[1])

            @when(t == 15)
            def _():
                relay_via(lag, c).wait_recv()
                go(functools.partial(pass_via, lag), c)

        if name in ("R2", "R3", "R4"):
            take_and_relay(there, int(name[1]) - 1, int(name[1]), c)
        if name in ("R5", "R6"):
            take_and_relay(there, int(name[1]) + 1, int(name[1]), c)
        if name == "W":
            take_and_relay(there, 4, None, c)
            take_and_relay(there, 5, None, c)

            @pl.when(there)
            def _():
                load_left(c)

        if name == "KA":

            @pl.when(there)
            def _():
                add_partner(0, 1, c)
                for way in range(2):
                    go(functools.partial(a_copy, way), c)

        if name == "KB":

            @pl.when(there)
            def _():
                add_partner(1, 2, c)
                for way in range(2):
                    go(functools.partial(b_copy, way), c)

        if name == "K0":

            @pl.when(there)
            def _():
                add_partner(3, 1, c)

        if name == "C":

            @pl.when(there)
            def _():
                remote(a_in.at[c], a_in.at[c], a_send.at[0, 0], a_recv.at[c], left).wait_recv()
                for way in range(2):
                    own[c, 1 + way, way] = own[c, 1 + way, way] + a_in[c, way]
                    go(functools.partial(c_copy, way), c)

        if name == "X":

            @pl.when(there)
            def _():
                remote(bc_in.at[c], bc_in.at[c], b_send.at[0, 0], bc_recv.at[c], left).wait_recv()
                own[c, 3, 0] = own[c, 3, 0] + (bc_in[c, 2] + bc_in[c, 1])
                own[c, 3, 1] = own[c, 3, 1] + (bc_in[c, 0] + bc_in[c, 3])
                go(y_copy, c)

        if name == "F":

            @pl.when(there)
            def _():
                y_copy(c).wait_recv()
                total = own[c, 3, yh] + y_in[c]
                out_ref[:, pl.ds(pl.multiple_of(c * W, W), W)] = total.T

    first = ZERO + min(AT.values()) // 4
    last = ZERO + CH + max(AT.values()) // 4

    def step(s, carry):
        for slot in range(4):
            for name in PLAN:
                if AT[name] % 4 == slot:
                    run(name, s - AT[name] // 4)

            @pl.when(inside(s))
            def _():
                multiply(slot, chunk_of(s))

            turn = s * 4 + slot
            base = max(first, ZERO - 4) * 4

            @pl.when((turn >= base) & (turn < base + keep))
            def _():
                prepare(jnp.clip(turn, base, base + keep - 1) - base)

        return carry

    lax.fori_loop(first, last + 1, step, 0)

    for c in (CH - 2, CH - 1):
        ends = [(relays(1), send_own_up)]
        for lag in range(2, keep):
            if lag != 7 and comes(lag):
                ends.append((relays(lag), functools.partial(relay, lag)))
        for lag in by_via:
            ends += [(t == 7, functools.partial(relay_via, lag)), (t == 15, functools.partial(pass_via, lag))]
        if downs:
            ends += [(t <= 10, send_own_far), ((t == 1) | (t == 2), send_own_seven)]
        for there, make in ends:

            @pl.when(there)
            def _():
                make(c).wait_send()

        for q in range(4):
            to_partner(q, c).wait_send()
        for way in range(2):
            for make in (a_copy, b_copy, c_copy):
                make(way, c).wait_send()
        y_copy(c).wait_send()


def collide(keep, memory, startup_cut, weight_index, weight_table, history, self_energy):
    smem = pl.BlockSpec(memory_space=pltpu.SMEM)
    vmem = pl.BlockSpec(memory_space=pltpu.VMEM)
    dma = pltpu.SemaphoreType.DMA
    piece = (W, W)
    return pl.pallas_call(
        functools.partial(kernel, keep),
        out_shape=jax.ShapeDtypeStruct((W, CH * W), F32),
        in_specs=[smem, smem, smem, smem, vmem, pl.BlockSpec(memory_space=pl.ANY)],
        out_specs=vmem,
        scratch_shapes=[
            pltpu.VMEM((keep, 2, 64, 2048), F32),
            pltpu.VMEM((2 * keep * W, 2048), BF16),
            pltpu.VMEM((CH, *piece), F32),
            pltpu.VMEM((keep, CH, *piece), F32),
            pltpu.VMEM((2, CH, *piece), F32),
            pltpu.VMEM((2 * W, keep * W), BF16),
            pltpu.VMEM((CH, 4, 2, *piece), F32),
            pltpu.VMEM((CH, 4, 2, *piece), F32),
            pltpu.VMEM((CH, 4, 2, *piece), F32),
            pltpu.VMEM((CH, 2, *piece), F32),
            pltpu.VMEM((CH, 4, *piece), F32),
            pltpu.VMEM((CH, *piece), F32),
            dma((keep,)),
            dma((keep, 2)), dma((keep, CH)), dma((2, CH)),
            dma((4, 2)), dma((3, CH)),
            dma((2, 2)), dma((CH,)),
            dma((2, 2)), dma((2, 2)), dma((CH,)),
            dma((2,)), dma((CH,)),
        ],
        compiler_params=pltpu.CompilerParams(
            collective_id=keep, has_side_effects=True, vmem_limit_bytes=60 * 1024 * 1024
        ),
        name=f"collision{keep}",
    )(memory, startup_cut, weight_index, weight_table, history, self_energy)


def local(self_energy, history, memory, startup_cut, weight_index, weight_table):
    keeps = tuple(PLANS)
    which = sum((memory[0] > keep).astype(jnp.int32) for keep in keeps[:-1])
    out = lax.switch(
        which,
        [functools.partial(collide, keep) for keep in keeps],
        memory, startup_cut, weight_index, weight_table, history.reshape(2 * 64, 1024), self_energy,
    )
    return out[None]


def solution(mesh):
    in_specs = (
        P("tm", None, None, "orb", None),
        P("tm", None, "orb", None),
        P(),
        P("tm"),
        P("tm", None),
        P(),
    )
    out_specs = P("tm", "orb", None)
    return jax.shard_map(local, mesh=mesh, in_specs=in_specs, out_specs=out_specs, check_vma=False)
```

```python
import functools

import jax
import jax.numpy as jnp
from jax import lax
from jax.experimental import pallas as pl
from jax.experimental.pallas import tpu as pltpu
from jax.sharding import PartitionSpec as P

F32 = jnp.float32
BF16 = jnp.bfloat16
MESH = pl.DeviceIdType.MESH
NT = 16
LAGS = 8
CH = 8
W = 128
ZERO = 16
ORDER = (2, 1, 3, 0)
PLANS = {
    3: (
        {
            "S1": -10, "R2": -5, "R3": 0, "W": 0, "KA": 3, "KB": 4, "K0": 8, "C": 7,
            "X": 12, "F": 18,
        },
        ("F", "X", "R3", "KA", "C", "R2", "S1", "W", "K0", "KB"),
    ),
    4: (
        {
            "S1": -14, "R2": -10, "R3": -5, "R4": 0, "P1": -11, "W": 0, "KA": 2, "KB": 4,
            "K0": 6, "C": 7, "X": 14, "F": 19,
        },
        ("S1", "C", "R2", "KB", "P1", "F", "K0", "R3", "X", "KA", "R4", "W"),
    ),
    5: (
        {
            "S1": -29, "R2": -14, "R3": -9, "R4": -5, "P1": -17, "P2": -12, "W": 0, "KA": 3,
            "KB": 4, "K0": 9, "C": 7, "X": 12, "F": 20,
        },
        ("F", "S1", "P1", "X", "KA", "P2", "R3", "R4", "KB", "R2", "C", "K0", "W"),
    ),
    8: (
        {
            "S1": -21, "D7": -13, "R2": -14, "R6": -8, "R3": -10, "R4": -5, "R5": -4, "P1": -22,
            "P2": -14, "W": 0, "KA": 2, "KB": 5, "K0": 10, "C": 7, "X": 13, "F": 17,
        },
        ("R2", "W", "C", "D7", "R4", "X", "KB", "R5", "F", "R6", "S1", "R3", "P2", "P1", "KA", "K0"),
    ),
}


def halves(value):
    high = value.astype(BF16)
    return high, (value - high.astype(F32)).astype(BF16)


def kernel(
    keep, mem_ref, cut_ref, index_ref, table_ref, hist_ref, se_ref, out_ref,
    stage, rhs, own_hist, gat, via, gx, own, oth, core_in, a_in, bc_in, y_in,
    se_sem, g_send, g_recv, v_recv, k_send, k_recv, a_send, a_recv, b_send, c_send, bc_recv, y_send, y_recv,
):
    ups = min(4, keep - 1)
    downs = keep > 5
    by_via = {3: (), 4: (1,)}.get(keep, (1, 2))
    AT, PLAN = PLANS[keep]
    t = lax.axis_index("tm")
    o = lax.axis_index("orb")
    yh, x, core = o // 8, (o // 2) % 4, o % 2

    def orb_of(yh_, x_, core_):
        return yh_ * 8 + x_ * 2 + core_

    up, down = t + 1, t - 1
    partner = (t, orb_of(yh, x, 1 - core))
    right = (t, orb_of(yh, (x + 1) % 4, core))
    left = (t, orb_of(yh, (x + 3) % 4, core))
    across = (t, orb_of(1 - yh, x, core))

    for lag in range(keep):
        pltpu.make_async_copy(se_ref.at[0, :, lag], stage.at[lag], se_sem.at[lag]).start()

    barrier = pltpu.get_barrier_semaphore()
    greet = [(t <= 14, t + 1), (t >= 1, t - 1)]
    if by_via:
        greet += [(t == 7, 15), (t == 15, 7), (t == 15, 8), (t == 8, 15)]
    if downs:
        greet += [
            (t <= 7, t + 7), ((t >= 7) & (t <= 14), t - 7),
            ((t == 9) | (t == 10), 15), (t == 15, 9), (t == 15, 10),
            ((t == 1) | (t == 2), 7), (t == 7, 1), (t == 7, 2),
        ]
    count = 4
    for there, who in greet:
        count = count + there.astype(jnp.int32)

        @pl.when(there)
        def _():
            pl.semaphore_signal(barrier, inc=1, device_id=(who, o), device_id_type=MESH)

    for who in (partner, right, left, across):
        pl.semaphore_signal(barrier, inc=1, device_id=who, device_id_type=MESH)

    for c in range(CH):
        own_hist[c] = hist_ref[:, c * W:(c + 1) * W].T
    for lag in range(1, keep):

        @pl.when(t < lag)
        def _():
            gat[lag] = jnp.zeros((CH, W, W), F32)

    pl.semaphore_wait(barrier, count)

    def remote(src, dst, send, recv, who):
        return pltpu.make_async_remote_copy(
            src_ref=src, dst_ref=dst, send_sem=send, recv_sem=recv, device_id=who, device_id_type=MESH
        )

    def go(make, c):
        @pl.when(c >= 2)
        def _():
            make(c - 2).wait_send()

        make(c).start()

    def history(src, lag, c, kind, who):
        return remote(src, gat.at[lag, c], g_send.at[kind, c % 2], g_recv.at[lag, c], (who, o))

    def send_own_up(c):
        return history(own_hist.at[c], 1, c, 1, up)

    def relay(lag, c):
        if lag <= 4:
            return history(gat.at[lag - 1, c], lag, c, lag, up)
        return history(gat.at[lag + 1, c], lag, c, lag, down)

    def send_own_far(c):
        return history(own_hist.at[c], 7 - jnp.maximum(t - 8, 0), c, 7, jnp.minimum(t + 7, 15))

    def send_own_seven(c):
        return history(own_hist.at[c], 7 - t, c, 6, 7)

    def relay_via(lag, c):
        src = own_hist.at[c] if lag == 1 else gat.at[1, c]
        return remote(src, via.at[lag - 1, c], g_send.at[lag, c % 2], v_recv.at[lag - 1, c], (15, o))

    def pass_via(lag, c):
        return history(via.at[lag - 1, c], lag, c, lag, 8)

    def comes(lag):
        return lag <= ups if lag <= 4 else downs

    def relays(lag):
        if lag >= 5:
            return (t - 1 >= lag) & (t != 8)
        if lag in by_via:
            return (t <= 14) & (t + 1 >= lag) & (t != 7)
        return (t <= 14) & (t + 1 >= lag)

    def arrived(lag, c):
        remote(gat.at[lag, c], gat.at[lag, c], g_send.at[lag, 0], g_recv.at[lag, c], partner).wait_recv()

    def inside(at):
        return (at >= ZERO) & (at < ZERO + CH)

    def chunk_of(at):
        return jnp.clip(at, ZERO, ZERO + CH - 1) - ZERO

    def take_and_relay(there, lag, nxt, c):
        if comes(lag):

            @pl.when(there & (t >= lag))
            def _():
                arrived(lag, c)

        if nxt is not None and comes(nxt):

            @pl.when(there & relays(nxt))
            def _():
                go(functools.partial(relay, nxt), c)

            if nxt in by_via:

                @pl.when(there & (t == 7))
                def _():
                    go(functools.partial(relay_via, nxt), c)

    def to_partner(q, c):
        return remote(oth.at[c, q], core_in.at[c, q], k_send.at[q, c % 2], k_recv.at[(0, 1, 1, 2)[q], c], partner)

    def add_partner(start, size, c):
        part = core_in.at[c, pl.ds(start, size)]
        remote(part, part, k_send.at[start, c % 2], k_recv.at[(0, 1, 1, 2)[start], c], partner).wait_recv()
        own[c, pl.ds(start, size)] = own[c, pl.ds(start, size)] + core_in[c, pl.ds(start, size)]

    def a_copy(way, c):
        return remote(own.at[c, 0, way], a_in.at[c, way], a_send.at[way, c % 2], a_recv.at[c], (right, left)[way])

    def b_copy(way, c):
        return remote(
            own.at[c, 1 + way, 1 - way], bc_in.at[c, way], b_send.at[way, c % 2], bc_recv.at[c], (right, left)[way]
        )

    def c_copy(way, c):
        return remote(
            own.at[c, 1 + way, way], bc_in.at[c, 2 + way], c_send.at[way, c % 2], bc_recv.at[c], (right, left)[way]
        )

    def y_copy(c):
        return remote(own.at[c, 3, 1 - yh], y_in.at[c], y_send.at[c % 2], y_recv.at[c], across)

    def prepare(lag):
        pltpu.make_async_copy(se_ref.at[0, :, lag], stage.at[lag], se_sem.at[lag]).wait()
        weight = table_ref[index_ref[0, lag]]
        last = mem_ref[0] - 1
        base = pl.multiple_of(lag * W, W)
        low_base = pl.multiple_of(keep * W + lag * W, W)
        for q, d in enumerate(ORDER):
            for side in range(2):
                for yh_ in range(2):
                    col = pl.multiple_of(yh_ * 1024 + ((x + d) % 4) * 256 + (core if side == 0 else 1 - core) * W, W)
                    rows = col + lax.broadcasted_iota(jnp.int32, (64, W), 1)
                    kept = (lag < last) | ((lag == last) & (rows >= cut_ref[0]))
                    coef = jnp.where(kept, weight, F32(0.0))
                    place = pl.ds((q * 4 + side * 2 + yh_) * W, W)
                    value = jnp.concatenate(
                        [stage[lag, 0, :, pl.ds(col, W)] * coef, -(stage[lag, 1, :, pl.ds(col, W)] * coef)], axis=0
                    )
                    high, low = halves(value)
                    rhs[pl.ds(base, W), place] = high
                    rhs[pl.ds(low_base, W), place] = low

    def load_left(c):
        for lag in range(keep):
            high, low = halves(own_hist[c] if lag == 0 else gat[lag, c])
            gx[:W, lag * W:(lag + 1) * W] = high
            gx[W:, lag * W:(lag + 1) * W] = low

    def multiply(q, c):
        cols = pl.ds(q * 512, 512)
        both = jnp.dot(gx[...], rhs[:keep * W, cols], preferred_element_type=F32)
        more = jnp.dot(gx[:W], rhs[keep * W:, cols], preferred_element_type=F32)
        total = both[:W] + both[W:] + more
        for yh_ in range(2):
            own[c, q, yh_] = total[:, yh_ * W:(yh_ + 1) * W]
            oth[c, q, yh_] = total[:, (2 + yh_) * W:(3 + yh_) * W]
        go(functools.partial(to_partner, q), c)

    def run(name, at):
        there = inside(at)
        c = chunk_of(at)

        def when(cond):
            return pl.when(there & cond)

        if name == "S1":

            @when(relays(1))
            def _():
                go(send_own_up, c)

            if 1 in by_via:

                @when(t == 7)
                def _():
                    go(functools.partial(relay_via, 1), c)

        if name == "D7" and downs:

            @when(t <= 10)
            def _():
                go(send_own_far, c)

            @when((t == 1) | (t == 2))
            def _():
                go(send_own_seven, c)

        if name in ("P1", "P2") and int(name[1]) in by_via:
            lag = int(name[1])

            @when(t == 15)
            def _():
                relay_via(lag, c).wait_recv()
                go(functools.partial(pass_via, lag), c)

        if name in ("R2", "R3", "R4"):
            take_and_relay(there, int(name[1]) - 1, int(name[1]), c)
        if name in ("R5", "R6"):
            take_and_relay(there, int(name[1]) + 1, int(name[1]), c)
        if name == "W":
            take_and_relay(there, 4, None, c)
            take_and_relay(there, 5, None, c)

            @pl.when(there)
            def _():
                load_left(c)

        if name == "KA":

            @pl.when(there)
            def _():
                add_partner(0, 1, c)
                for way in range(2):
                    go(functools.partial(a_copy, way), c)

        if name == "KB":

            @pl.when(there)
            def _():
                add_partner(1, 2, c)
                for way in range(2):
                    go(functools.partial(b_copy, way), c)

        if name == "K0":

            @pl.when(there)
            def _():
                add_partner(3, 1, c)

        if name == "C":

            @pl.when(there)
            def _():
                remote(a_in.at[c], a_in.at[c], a_send.at[0, 0], a_recv.at[c], left).wait_recv()
                for way in range(2):
                    own[c, 1 + way, way] = own[c, 1 + way, way] + a_in[c, way]
                    go(functools.partial(c_copy, way), c)

        if name == "X":

            @pl.when(there)
            def _():
                remote(bc_in.at[c], bc_in.at[c], b_send.at[0, 0], bc_recv.at[c], left).wait_recv()
                own[c, 3, 0] = own[c, 3, 0] + (bc_in[c, 2] + bc_in[c, 1])
                own[c, 3, 1] = own[c, 3, 1] + (bc_in[c, 0] + bc_in[c, 3])
                go(y_copy, c)

        if name == "F":

            @pl.when(there)
            def _():
                y_copy(c).wait_recv()
                total = own[c, 3, yh] + y_in[c]
                out_ref[:, pl.ds(pl.multiple_of(c * W, W), W)] = total.T

    first = ZERO + min(AT.values()) // 4
    last = ZERO + CH + max(AT.values()) // 4

    def step(s, carry):
        for slot in range(4):
            for name in PLAN:
                if AT[name] % 4 == slot:
                    run(name, s - AT[name] // 4)

            @pl.when(inside(s))
            def _():
                multiply(slot, chunk_of(s))

            turn = s * 4 + slot
            base = max(first, ZERO - 4) * 4

            @pl.when((turn >= base) & (turn < base + keep))
            def _():
                prepare(jnp.clip(turn, base, base + keep - 1) - base)

        return carry

    lax.fori_loop(first, last + 1, step, 0)

    for c in (CH - 2, CH - 1):
        ends = [(relays(1), send_own_up)]
        for lag in range(2, keep):
            if lag != 7 and comes(lag):
                ends.append((relays(lag), functools.partial(relay, lag)))
        for lag in by_via:
            ends += [(t == 7, functools.partial(relay_via, lag)), (t == 15, functools.partial(pass_via, lag))]
        if downs:
            ends += [(t <= 10, send_own_far), ((t == 1) | (t == 2), send_own_seven)]
        for there, make in ends:

            @pl.when(there)
            def _():
                make(c).wait_send()

        for q in range(4):
            to_partner(q, c).wait_send()
        for way in range(2):
            for make in (a_copy, b_copy, c_copy):
                make(way, c).wait_send()
        y_copy(c).wait_send()


def collide(keep, memory, startup_cut, weight_index, weight_table, history, self_energy):
    smem = pl.BlockSpec(memory_space=pltpu.SMEM)
    vmem = pl.BlockSpec(memory_space=pltpu.VMEM)
    dma = pltpu.SemaphoreType.DMA
    piece = (W, W)
    return pl.pallas_call(
        functools.partial(kernel, keep),
        out_shape=jax.ShapeDtypeStruct((W, CH * W), F32),
        in_specs=[smem, smem, smem, smem, vmem, pl.BlockSpec(memory_space=pl.ANY)],
        out_specs=vmem,
        scratch_shapes=[
            pltpu.VMEM((keep, 2, 64, 2048), F32),
            pltpu.VMEM((2 * keep * W, 2048), BF16),
            pltpu.VMEM((CH, *piece), F32),
            pltpu.VMEM((keep, CH, *piece), F32),
            pltpu.VMEM((2, CH, *piece), F32),
            pltpu.VMEM((2 * W, keep * W), BF16),
            pltpu.VMEM((CH, 4, 2, *piece), F32),
            pltpu.VMEM((CH, 4, 2, *piece), F32),
            pltpu.VMEM((CH, 4, 2, *piece), F32),
            pltpu.VMEM((CH, 2, *piece), F32),
            pltpu.VMEM((CH, 4, *piece), F32),
            pltpu.VMEM((CH, *piece), F32),
            dma((keep,)),
            dma((keep, 2)), dma((keep, CH)), dma((2, CH)),
            dma((4, 2)), dma((3, CH)),
            dma((2, 2)), dma((CH,)),
            dma((2, 2)), dma((2, 2)), dma((CH,)),
            dma((2,)), dma((CH,)),
        ],
        compiler_params=pltpu.CompilerParams(
            collective_id=keep, has_side_effects=True, vmem_limit_bytes=60 * 1024 * 1024
        ),
        name=f"collision{keep}",
    )(memory, startup_cut, weight_index, weight_table, history, self_energy)


def local(self_energy, history, memory, startup_cut, weight_index, weight_table):
    keeps = tuple(PLANS)
    which = sum((memory[0] > keep).astype(jnp.int32) for keep in keeps[:-1])
    out = lax.switch(
        which,
        [functools.partial(collide, keep) for keep in keeps],
        memory, startup_cut, weight_index, weight_table, history.reshape(2 * 64, 1024), self_energy,
    )
    return out[None]


def solution(mesh):
    in_specs = (
        P("tm", None, None, "orb", None),
        P("tm", None, "orb", None),
        P(),
        P("tm"),
        P("tm", None),
        P(),
    )
    out_specs = P("tm", "orb", None)
    return jax.shard_map(local, mesh=mesh, in_specs=in_specs, out_specs=out_specs, check_vma=False)
```

```python
import functools

import jax
import jax.numpy as jnp
from jax import lax
from jax.experimental import pallas as pl
from jax.experimental.pallas import tpu as pltpu
from jax.sharding import PartitionSpec as P

F32 = jnp.float32
BF16 = jnp.bfloat16
MESH = pl.DeviceIdType.MESH
NT = 16
LAGS = 8
CH = 8
W = 128
ZERO = 16
ORDER = (2, 1, 3, 0)
PLANS = {
    3: (
        {
            "S1": -10, "R2": -5, "R3": 0, "W": 0, "KA": 3, "KB": 4, "K0": 8, "C": 7,
            "X": 12, "F": 18,
        },
        ("F", "X", "R3", "KA", "C", "R2", "S1", "W", "K0", "KB"),
    ),
    4: (
        {
            "S1": -14, "R2": -10, "R3": -5, "R4": 0, "P1": -11, "W": 0, "KA": 2, "KB": 4,
            "K0": 6, "C": 7, "X": 14, "F": 19,
        },
        ("S1", "C", "R2", "KB", "P1", "F", "K0", "R3", "X", "KA", "R4", "W"),
    ),
    5: (
        {
            "S1": -29, "R2": -14, "R3": -9, "R4": -5, "P1": -17, "P2": -12, "W": 0, "KA": 3,
            "KB": 4, "K0": 9, "C": 7, "X": 12, "F": 20,
        },
        ("F", "S1", "P1", "X", "KA", "P2", "R3", "R4", "KB", "R2", "C", "K0", "W"),
    ),
    8: (
        {
            "S1": -20, "D7": -12, "R2": -14, "R6": -6, "R3": -10, "R4": -5, "R5": -3, "P1": -18,
            "P2": -11, "W": 0, "KA": 2, "KB": 5, "K0": 9, "C": 6, "X": 14, "F": 18,
        },
        ("S1", "R4", "X", "F", "D7", "R2", "KA", "R6", "P1", "C", "KB", "R3", "K0", "P2", "R5", "W"),
    ),
}


def halves(value):
    high = value.astype(BF16)
    return high, (value - high.astype(F32)).astype(BF16)


def kernel(
    keep, mem_ref, cut_ref, index_ref, table_ref, hist_ref, se_ref, out_ref,
    stage, rhs, own_hist, gat, via, gx, own, oth, core_in, a_in, bc_in, y_in,
    se_sem, g_send, g_recv, v_recv, k_send, k_recv, a_send, a_recv, b_send, c_send, bc_recv, y_send, y_recv,
):
    ups = min(4, keep - 1)
    downs = keep > 5
    by_via = {3: (), 4: (1,)}.get(keep, (1, 2))
    AT, PLAN = PLANS[keep]
    t = lax.axis_index("tm")
    o = lax.axis_index("orb")
    yh, x, core = o // 8, (o // 2) % 4, o % 2

    def orb_of(yh_, x_, core_):
        return yh_ * 8 + x_ * 2 + core_

    up, down = t + 1, t - 1
    partner = (t, orb_of(yh, x, 1 - core))
    right = (t, orb_of(yh, (x + 1) % 4, core))
    left = (t, orb_of(yh, (x + 3) % 4, core))
    across = (t, orb_of(1 - yh, x, core))

    for lag in range(keep):
        pltpu.make_async_copy(se_ref.at[0, :, lag], stage.at[lag], se_sem.at[lag]).start()

    barrier = pltpu.get_barrier_semaphore()
    greet = [(t <= 14, t + 1), (t >= 1, t - 1)]
    if by_via:
        greet += [(t == 7, 15), (t == 15, 7), (t == 15, 8), (t == 8, 15)]
    if downs:
        greet += [
            (t <= 7, t + 7), ((t >= 7) & (t <= 14), t - 7),
            ((t == 9) | (t == 10), 15), (t == 15, 9), (t == 15, 10),
            ((t == 1) | (t == 2), 7), (t == 7, 1), (t == 7, 2),
        ]
    count = 4
    for there, who in greet:
        count = count + there.astype(jnp.int32)

        @pl.when(there)
        def _():
            pl.semaphore_signal(barrier, inc=1, device_id=(who, o), device_id_type=MESH)

    for who in (partner, right, left, across):
        pl.semaphore_signal(barrier, inc=1, device_id=who, device_id_type=MESH)

    for c in range(CH):
        own_hist[c] = hist_ref[:, c * W:(c + 1) * W].T
    for lag in range(1, keep):

        @pl.when(t < lag)
        def _():
            gat[lag] = jnp.zeros((CH, W, W), F32)

    pl.semaphore_wait(barrier, count)

    def remote(src, dst, send, recv, who):
        return pltpu.make_async_remote_copy(
            src_ref=src, dst_ref=dst, send_sem=send, recv_sem=recv, device_id=who, device_id_type=MESH
        )

    def go(make, c):
        @pl.when(c >= 2)
        def _():
            make(c - 2).wait_send()

        make(c).start()

    def history(src, lag, c, kind, who):
        return remote(src, gat.at[lag, c], g_send.at[kind, c % 2], g_recv.at[lag, c], (who, o))

    def send_own_up(c):
        return history(own_hist.at[c], 1, c, 1, up)

    def relay(lag, c):
        if lag <= 4:
            return history(gat.at[lag - 1, c], lag, c, lag, up)
        return history(gat.at[lag + 1, c], lag, c, lag, down)

    def send_own_far(c):
        return history(own_hist.at[c], 7 - jnp.maximum(t - 8, 0), c, 7, jnp.minimum(t + 7, 15))

    def send_own_seven(c):
        return history(own_hist.at[c], 7 - t, c, 6, 7)

    def relay_via(lag, c):
        src = own_hist.at[c] if lag == 1 else gat.at[1, c]
        return remote(src, via.at[lag - 1, c], g_send.at[lag, c % 2], v_recv.at[lag - 1, c], (15, o))

    def pass_via(lag, c):
        return history(via.at[lag - 1, c], lag, c, lag, 8)

    def comes(lag):
        return lag <= ups if lag <= 4 else downs

    def relays(lag):
        if lag >= 5:
            return (t - 1 >= lag) & (t != 8)
        if lag in by_via:
            return (t <= 14) & (t + 1 >= lag) & (t != 7)
        return (t <= 14) & (t + 1 >= lag)

    def arrived(lag, c):
        remote(gat.at[lag, c], gat.at[lag, c], g_send.at[lag, 0], g_recv.at[lag, c], partner).wait_recv()

    def inside(at):
        return (at >= ZERO) & (at < ZERO + CH)

    def chunk_of(at):
        return jnp.clip(at, ZERO, ZERO + CH - 1) - ZERO

    def take_and_relay(there, lag, nxt, c):
        if comes(lag):

            @pl.when(there & (t >= lag))
            def _():
                arrived(lag, c)

        if nxt is not None and comes(nxt):

            @pl.when(there & relays(nxt))
            def _():
                go(functools.partial(relay, nxt), c)

            if nxt in by_via:

                @pl.when(there & (t == 7))
                def _():
                    go(functools.partial(relay_via, nxt), c)

    def to_partner(q, c):
        return remote(oth.at[c, q], core_in.at[c, q], k_send.at[q, c % 2], k_recv.at[(0, 1, 1, 2)[q], c], partner)

    def add_partner(start, size, c):
        part = core_in.at[c, pl.ds(start, size)]
        remote(part, part, k_send.at[start, c % 2], k_recv.at[(0, 1, 1, 2)[start], c], partner).wait_recv()
        own[c, pl.ds(start, size)] = own[c, pl.ds(start, size)] + core_in[c, pl.ds(start, size)]

    def a_copy(way, c):
        return remote(own.at[c, 0, way], a_in.at[c, way], a_send.at[way, c % 2], a_recv.at[c], (right, left)[way])

    def b_copy(way, c):
        return remote(
            own.at[c, 1 + way, 1 - way], bc_in.at[c, way], b_send.at[way, c % 2], bc_recv.at[c], (right, left)[way]
        )

    def c_copy(way, c):
        return remote(
            own.at[c, 1 + way, way], bc_in.at[c, 2 + way], c_send.at[way, c % 2], bc_recv.at[c], (right, left)[way]
        )

    def y_copy(c):
        return remote(own.at[c, 3, 1 - yh], y_in.at[c], y_send.at[c % 2], y_recv.at[c], across)

    def prepare(lag):
        pltpu.make_async_copy(se_ref.at[0, :, lag], stage.at[lag], se_sem.at[lag]).wait()
        weight = table_ref[index_ref[0, lag]]
        last = mem_ref[0] - 1
        base = pl.multiple_of(lag * W, W)
        low_base = pl.multiple_of(keep * W + lag * W, W)
        for q, d in enumerate(ORDER):
            for side in range(2):
                for yh_ in range(2):
                    col = pl.multiple_of(yh_ * 1024 + ((x + d) % 4) * 256 + (core if side == 0 else 1 - core) * W, W)
                    rows = col + lax.broadcasted_iota(jnp.int32, (64, W), 1)
                    kept = (lag < last) | ((lag == last) & (rows >= cut_ref[0]))
                    coef = jnp.where(kept, weight, F32(0.0))
                    place = pl.ds((q * 4 + side * 2 + yh_) * W, W)
                    value = jnp.concatenate(
                        [stage[lag, 0, :, pl.ds(col, W)] * coef, -(stage[lag, 1, :, pl.ds(col, W)] * coef)], axis=0
                    )
                    high, low = halves(value)
                    rhs[pl.ds(base, W), place] = high
                    rhs[pl.ds(low_base, W), place] = low

    def load_left(c):
        for lag in range(keep):
            high, low = halves(own_hist[c] if lag == 0 else gat[lag, c])
            gx[:W, lag * W:(lag + 1) * W] = high
            gx[W:, lag * W:(lag + 1) * W] = low

    def multiply(q, c):
        cols = pl.ds(q * 512, 512)
        both = jnp.dot(gx[...], rhs[:keep * W, cols], preferred_element_type=F32)
        more = jnp.dot(gx[:W], rhs[keep * W:, cols], preferred_element_type=F32)
        total = both[:W] + both[W:] + more
        for yh_ in range(2):
            own[c, q, yh_] = total[:, yh_ * W:(yh_ + 1) * W]
            oth[c, q, yh_] = total[:, (2 + yh_) * W:(3 + yh_) * W]
        go(functools.partial(to_partner, q), c)

    def run(name, at):
        there = inside(at)
        c = chunk_of(at)

        def when(cond):
            return pl.when(there & cond)

        if name == "S1":

            @when(relays(1))
            def _():
                go(send_own_up, c)

            if 1 in by_via:

                @when(t == 7)
                def _():
                    go(functools.partial(relay_via, 1), c)

        if name == "D7" and downs:

            @when(t <= 10)
            def _():
                go(send_own_far, c)

            @when((t == 1) | (t == 2))
            def _():
                go(send_own_seven, c)

        if name in ("P1", "P2") and int(name[1]) in by_via:
            lag = int(name[1])

            @when(t == 15)
            def _():
                relay_via(lag, c).wait_recv()
                go(functools.partial(pass_via, lag), c)

        if name in ("R2", "R3", "R4"):
            take_and_relay(there, int(name[1]) - 1, int(name[1]), c)
        if name in ("R5", "R6"):
            take_and_relay(there, int(name[1]) + 1, int(name[1]), c)
        if name == "W":
            take_and_relay(there, 4, None, c)
            take_and_relay(there, 5, None, c)

            @pl.when(there)
            def _():
                load_left(c)

        if name == "KA":

            @pl.when(there)
            def _():
                add_partner(0, 1, c)
                for way in range(2):
                    go(functools.partial(a_copy, way), c)

        if name == "KB":

            @pl.when(there)
            def _():
                add_partner(1, 2, c)
                for way in range(2):
                    go(functools.partial(b_copy, way), c)

        if name == "K0":

            @pl.when(there)
            def _():
                add_partner(3, 1, c)

        if name == "C":

            @pl.when(there)
            def _():
                remote(a_in.at[c], a_in.at[c], a_send.at[0, 0], a_recv.at[c], left).wait_recv()
                for way in range(2):
                    own[c, 1 + way, way] = own[c, 1 + way, way] + a_in[c, way]
                    go(functools.partial(c_copy, way), c)

        if name == "X":

            @pl.when(there)
            def _():
                remote(bc_in.at[c], bc_in.at[c], b_send.at[0, 0], bc_recv.at[c], left).wait_recv()
                own[c, 3, 0] = own[c, 3, 0] + (bc_in[c, 2] + bc_in[c, 1])
                own[c, 3, 1] = own[c, 3, 1] + (bc_in[c, 0] + bc_in[c, 3])
                go(y_copy, c)

        if name == "F":

            @pl.when(there)
            def _():
                y_copy(c).wait_recv()
                total = own[c, 3, yh] + y_in[c]
                out_ref[:, pl.ds(pl.multiple_of(c * W, W), W)] = total.T

    first = ZERO + min(AT.values()) // 4
    last = ZERO + CH + max(AT.values()) // 4

    def step(s, carry):
        for slot in range(4):
            for name in PLAN:
                if AT[name] % 4 == slot:
                    run(name, s - AT[name] // 4)

            @pl.when(inside(s))
            def _():
                multiply(slot, chunk_of(s))

            turn = s * 4 + slot
            base = max(first, ZERO - 4) * 4

            @pl.when((turn >= base) & (turn < base + keep))
            def _():
                prepare(jnp.clip(turn, base, base + keep - 1) - base)

        return carry

    lax.fori_loop(first, last + 1, step, 0)

    for c in (CH - 2, CH - 1):
        ends = [(relays(1), send_own_up)]
        for lag in range(2, keep):
            if lag != 7 and comes(lag):
                ends.append((relays(lag), functools.partial(relay, lag)))
        for lag in by_via:
            ends += [(t == 7, functools.partial(relay_via, lag)), (t == 15, functools.partial(pass_via, lag))]
        if downs:
            ends += [(t <= 10, send_own_far), ((t == 1) | (t == 2), send_own_seven)]
        for there, make in ends:

            @pl.when(there)
            def _():
                make(c).wait_send()

        for q in range(4):
            to_partner(q, c).wait_send()
        for way in range(2):
            for make in (a_copy, b_copy, c_copy):
                make(way, c).wait_send()
        y_copy(c).wait_send()


def collide(keep, memory, startup_cut, weight_index, weight_table, history, self_energy):
    smem = pl.BlockSpec(memory_space=pltpu.SMEM)
    vmem = pl.BlockSpec(memory_space=pltpu.VMEM)
    dma = pltpu.SemaphoreType.DMA
    piece = (W, W)
    return pl.pallas_call(
        functools.partial(kernel, keep),
        out_shape=jax.ShapeDtypeStruct((W, CH * W), F32),
        in_specs=[smem, smem, smem, smem, vmem, pl.BlockSpec(memory_space=pl.ANY)],
        out_specs=vmem,
        scratch_shapes=[
            pltpu.VMEM((keep, 2, 64, 2048), F32),
            pltpu.VMEM((2 * keep * W, 2048), BF16),
            pltpu.VMEM((CH, *piece), F32),
            pltpu.VMEM((keep, CH, *piece), F32),
            pltpu.VMEM((2, CH, *piece), F32),
            pltpu.VMEM((2 * W, keep * W), BF16),
            pltpu.VMEM((CH, 4, 2, *piece), F32),
            pltpu.VMEM((CH, 4, 2, *piece), F32),
            pltpu.VMEM((CH, 4, 2, *piece), F32),
            pltpu.VMEM((CH, 2, *piece), F32),
            pltpu.VMEM((CH, 4, *piece), F32),
            pltpu.VMEM((CH, *piece), F32),
            dma((keep,)),
            dma((keep, 2)), dma((keep, CH)), dma((2, CH)),
            dma((4, 2)), dma((3, CH)),
            dma((2, 2)), dma((CH,)),
            dma((2, 2)), dma((2, 2)), dma((CH,)),
            dma((2,)), dma((CH,)),
        ],
        compiler_params=pltpu.CompilerParams(
            collective_id=keep, has_side_effects=True, vmem_limit_bytes=60 * 1024 * 1024
        ),
        name=f"collision{keep}",
    )(memory, startup_cut, weight_index, weight_table, history, self_energy)


def local(self_energy, history, memory, startup_cut, weight_index, weight_table):
    keeps = tuple(PLANS)
    which = sum((memory[0] > keep).astype(jnp.int32) for keep in keeps[:-1])
    out = lax.switch(
        which,
        [functools.partial(collide, keep) for keep in keeps],
        memory, startup_cut, weight_index, weight_table, history.reshape(2 * 64, 1024), self_energy,
    )
    return out[None]


def solution(mesh):
    in_specs = (
        P("tm", None, None, "orb", None),
        P("tm", None, "orb", None),
        P(),
        P("tm"),
        P("tm", None),
        P(),
    )
    out_specs = P("tm", "orb", None)
    return jax.shard_map(local, mesh=mesh, in_specs=in_specs, out_specs=out_specs, check_vma=False)
```
